32 devices in a mesh: dp: 4 (over y, core), ctx: 8 (over z, x).
Axes of the slice: x: 2, y: 2, z: 4, core: 2. Of those that a mesh axis runs over, the one named last changes fastest.
Arguments:
- queries: bfloat16 [4608, 256], P(('dp', 'ctx')), parts along dimension 0, may hold values from -5 to 5
- keys: bfloat16 [4608, 256], P(('dp', 'ctx')), parts along dimension 0, may hold values from -5 to 5
- values: bfloat16 [4608, 256], P(('dp', 'ctx')), parts along dimension 0, may hold values from -2.5 to 2.5
- out_grad: bfloat16 [4608, 256], P(('dp', 'ctx')), parts along dimension 0, may hold values from -5 to 5
- span_end: int32 [4608], P(('dp', 'ctx')), parts along dimension 0, may hold values from 0 to 1152, as said below
Outputs:
- output: bfloat16 [4608, 256], P(('dp', 'ctx')), parts along dimension 0
- query_grad: float32 [4608, 256], P(('dp', 'ctx')), parts along dimension 0
- key_grad: float32 [4608, 256], P(('dp', 'ctx')), parts along dimension 0
- value_grad: float32 [4608, 256], P(('dp', 'ctx')), parts along dimension 0
The draws below stay inside these ranges and needn't reach their ends.
There are 4 independent parts, one for each index of `dp`. The reference program is written for one: setup_inputs(seed, part) draws one part's arguments, and reference() takes and returns one part's arrays. A program takes and returns all parts, laid end to end along the dimension named above; each array names one. Nothing has to cross between parts.
Inputs may be any that keep to these rules, and one draw needn't show every extreme that they name: `span_end`: image spans are runs of consecutive tokens, each of at most 288 tokens; every token of a span holds the position just past the span's last token; the last 288 tokens of a document form one span.
All inputs are finite; a program needn't handle non-finite values.
Results may differ from the reference program's by a relative error of at most 0.035.
Values may be sent and summed in bfloat16 or wider, within the bound.
A program may use at most 64 MiB of HBM per device.

```python
import math
import jax
import jax.numpy as jnp
from jax import lax

HEADS = 2
HEAD_DIM = 128
FEATURES = 256
TOKENS = 1152
IMG = 288


def draw_queries(key, part):
    width = HEADS * HEAD_DIM
    drawn = jnp.clip(jax.random.normal(jax.random.fold_in(key, 11), (TOKENS, width), jnp.float32), -4.0, 4.0)
    return drawn.astype(jnp.bfloat16)


def draw_keys(key, part):
    width = HEADS * HEAD_DIM
    drawn = jnp.clip(jax.random.normal(jax.random.fold_in(key, 31), (TOKENS, width), jnp.float32), -4.0, 4.0)
    return drawn.astype(jnp.bfloat16)


def draw_span_end(key, part):
    span_count = TOKENS // (IMG // 2) + 2
    gaps = jax.random.randint(jax.random.fold_in(key, 21), (span_count,), 0, IMG)
    lengths = jax.random.randint(jax.random.fold_in(key, 22), (span_count,), IMG // 2, IMG + 1)
    ends = jnp.cumsum(gaps + lengths)
    starts = ends - lengths
    kept = ends <= TOKENS - IMG - 1
    positions = jnp.arange(TOKENS, dtype=jnp.int32)
    inside = (positions[:, None] >= starts[None, :]) & (positions[:, None] < ends[None, :]) & kept[None, :]
    result = jnp.sum(jnp.where(inside, ends[None, :], 0), axis=1) + jnp.where(positions >= TOKENS - IMG, TOKENS, 0)
    return result.astype(jnp.int32)


def block_levels(stream_key, dims, pieces, smallest, top_value):
    level = 1.0
    for position, shards_of in pieces:
        heights = jax.random.uniform(jax.random.fold_in(jax.random.fold_in(stream_key, 6), position), (shards_of,), jnp.float32, smallest / len(pieces), top_value / len(pieces))
        level = level * jnp.repeat(jnp.exp(heights), dims[position] // shards_of).reshape((-1,) + (1,) * (len(dims) - 1 - position))
    return level


def gaussian(stream_key, extent, scale, limit, cuts=(), kind=jnp.bfloat16):
    entries = jax.random.normal(stream_key, extent, jnp.float32) * scale
    if len(cuts) > 0:
        entries = block_levels(stream_key, extent, cuts, -0.22, 0.18) * entries
    return jnp.clip(entries, min=-limit, max=limit).astype(kind)


def setup_inputs(seed: int = 0, part: int = 0) -> dict:
    arg_keys = jax.random.split(jax.random.key(seed), 6)
    part_splits = jax.random.split(jax.random.fold_in(arg_keys[5], part), 6)
    queries = draw_queries(jax.random.fold_in(jax.random.fold_in(arg_keys[5], part), 71), part)
    keys = draw_keys(jax.random.fold_in(jax.random.fold_in(arg_keys[5], part), 71), part)
    values = gaussian(part_splits[2], (TOKENS, FEATURES), 0.5, 2.5, ((0, 8),))
    out_grad = gaussian(part_splits[3], (TOKENS, FEATURES), 1.0, 5.0, ((0, 8),))
    span_end = draw_span_end(jax.random.fold_in(jax.random.fold_in(arg_keys[5], part), 71), part)
    return {"queries": queries, "keys": keys, "values": values, "out_grad": out_grad, "span_end": span_end}


def rounded(matrix):
    return lax.optimization_barrier(matrix.astype(jnp.bfloat16)).astype(jnp.float32)


def reference(queries, keys, values, out_grad, span_end):
    total_rows = queries.shape[0]
    scaling = HEAD_DIM ** -0.5
    query_all = queries.astype(jnp.float32).reshape(total_rows, HEADS, HEAD_DIM)
    key_all = keys.astype(jnp.float32).reshape(total_rows, HEADS, HEAD_DIM)
    value_all = values.astype(jnp.float32).reshape(total_rows, HEADS, HEAD_DIM)
    grad_all = out_grad.astype(jnp.float32).reshape(total_rows, HEADS, HEAD_DIM)
    positions = jnp.arange(total_rows, dtype=jnp.int32)
    limits = jnp.maximum(positions + 1, span_end.astype(jnp.int32))
    block_rows = math.gcd(512, total_rows)
    block_count = total_rows // block_rows

    def masked_scores(offset):
        query_block = lax.dynamic_slice_in_dim(query_all, offset, block_rows, 0)
        limit_block = lax.dynamic_slice_in_dim(limits, offset, block_rows, 0)
        scores = jnp.einsum("qhd,khd->hqk", query_block, key_all) * scaling
        visible = (positions[None, :] < limit_block[:, None])[None]
        return jnp.where(visible, scores, -jnp.inf)

    def forward_block(index):
        offset = index * block_rows
        scores = masked_scores(offset)
        highest = jnp.max(scores, axis=-1)
        log_total = highest + jnp.log(jnp.sum(jnp.exp(scores - highest[..., None]), axis=-1))
        probs = jnp.exp(scores - log_total[..., None])
        output = jnp.einsum("hqk,khd->qhd", probs, value_all,
                            precision=lax.Precision.HIGHEST).astype(jnp.bfloat16)
        return output, log_total

    indices = jnp.arange(block_count, dtype=jnp.int32)
    outputs, log_totals = lax.map(forward_block, indices)
    output_all = outputs.reshape(total_rows, HEADS, HEAD_DIM)

    def backward_block(totals, index):
        key_grad, value_grad = totals
        offset = index * block_rows
        query_block = lax.dynamic_slice_in_dim(query_all, offset, block_rows, 0)
        grad_block = lax.dynamic_slice_in_dim(grad_all, offset, block_rows, 0)
        output_block = lax.dynamic_slice_in_dim(output_all, offset, block_rows, 0).astype(jnp.float32)
        scores = masked_scores(offset)
        probs = jnp.exp(scores - log_totals[index][..., None])
        row_dot = jnp.sum(grad_block * output_block, axis=-1).T
        prob_grad = jnp.einsum("qhd,khd->hqk", grad_block, value_all)
        score_grad = rounded(probs * (prob_grad - row_dot[..., None]))
        query_grad = jnp.einsum("hqk,khd->qhd", score_grad, key_all) * scaling
        key_grad = key_grad + jnp.einsum("hqk,qhd->khd", score_grad, query_block)
        value_grad = value_grad + jnp.einsum("hqk,qhd->khd", rounded(probs), grad_block)
        return (key_grad, value_grad), query_grad

    zero_rows = jnp.zeros((total_rows, HEADS, HEAD_DIM), jnp.float32)
    grads, query_grads = lax.scan(backward_block, (zero_rows, zero_rows), indices)
    key_grad, value_grad = grads
    flat_shape = (total_rows, HEADS * HEAD_DIM)
    return (output_all.reshape(flat_shape),
            query_grads.reshape(flat_shape),
            (key_grad * scaling).reshape(flat_shape),
            value_grad.reshape(flat_shape))
```

```python
import functools

import jax
import jax.numpy as jnp
from jax import lax
from jax.experimental import pallas as pl
from jax.experimental.pallas import tpu as pltpu
from jax.sharding import PartitionSpec as P

HEADS = 2
HEAD_DIM = 128
IMG = 288
HIDDEN = -1e30
KEY, VALUE, QUERY, GRAD = range(4)


def dot(a, b, a_dim, b_dim):
    return lax.dot_general(a, b, (((a_dim,), (b_dim,)), ((), ())), preferred_element_type=jnp.float32)


def kernel(
    n, rows,
    q_in, k_in, v_in, g_in, ends_in,
    o_ref, dq_ref, dk_ref, dv_ref,
    buf, ends, pe, pd, pair_stats, st_in, st_out, total, fin,
    acc_o, acc_q, acc_k, acc_v, alt, ret_out, ret_in, res_out, res_in,
    local_sem, x_recv, z_recv, end_recv, st_recv, ret_recv, res_recv, sent, ready,
):
    scaling = HEAD_DIM ** -0.5
    blocks = n // HEADS
    span = HEADS * rows
    cut = blocks * span - IMG
    last = blocks - 1
    me = lax.axis_index("ctx")
    z = me // HEADS
    x = me % HEADS
    sources = (k_in, v_in, q_in, g_in)
    OUT, DQ, DK, DV = range(4)

    def device(block, column):
        return {"ctx": block * HEADS + column}

    def ahead(block):
        return ((block + 1) * span < cut) & (block + 1 < blocks)

    def rows_of(portion):
        return pl.ds(pl.multiple_of(portion * rows, 16), rows)

    def columns_of(head):
        return pl.ds(pl.multiple_of(head * HEAD_DIM, HEAD_DIM), HEAD_DIM)

    own_rows, other_rows = rows_of(x), rows_of(1 - x)
    own_columns, other_columns = columns_of(x), columns_of(1 - x)

    key_back = span < cut
    query_back = 2 * span < cut and last > 1
    prompt = (z != 1) | (lax.axis_index("dp") % 2 == 0)
    down_key = (z == 1) & ahead(0)
    up_query = (z >= 1) & ahead(z)

    def up_key(block):
        return (z + 1 < last) | ((z + 1 == last) & (block >= 2))

    def takes_part(block, target):
        return (target >= 1) & ((target <= block) | ((target == block + 1) & ahead(block)))

    barrier = pltpu.get_barrier_semaphore()
    for target in range(1, blocks):
        @pl.when(target > z)
        def _():
            for column in range(HEADS):
                pl.semaphore_signal(barrier, inc=1, device_id=device(target, column))
    pl.semaphore_signal(barrier, inc=1, device_id=device(z, 1 - x))

    def own_copy(array):
        return pltpu.make_async_copy(
            sources[array].at[:, own_columns], buf.at[array, z, own_rows], local_sem.at[0])

    for array in range(4):
        own_copy(array).start()
    pltpu.make_async_copy(ends_in, ends.at[x], local_sem.at[1]).start()

    pl.semaphore_wait(barrier, HEADS * z + 1)
    for target in range(last):
        @pl.when(target < z)
        def _():
            for column in range(HEADS):
                pl.semaphore_signal(ready.at[z], inc=1, device_id=device(target, column))

    def remote(src, dst, recv, target, column):
        return pltpu.make_async_remote_copy(
            src_ref=src, dst_ref=dst, send_sem=sent, recv_sem=recv, device_id=device(target, column))

    def array_copy(array, block, portion, target, own=False):
        dst = buf.at[array, block, rows_of(portion)]
        return remote(
            sources[array].at[:, own_columns] if own else dst, dst,
            z_recv.at[array // 2, block], target, x)

    def query_copy(array, target, column):
        return remote(
            sources[array].at[:, columns_of(column)], buf.at[array, z, own_rows],
            z_recv.at[array // 2, z], target, column)

    def x_copy(array):
        return remote(
            sources[array].at[:, other_columns], buf.at[array, z, own_rows], x_recv.at[array], z, 1 - x)

    def x_ends():
        return remote(ends_in, ends.at[x], x_recv.at[4], z, 1 - x)

    def up_ends(column):
        return remote(ends_in, ends.at[HEADS + x], end_recv, z + 1, column)

    def landed(ref, sem):
        pltpu.make_async_copy(ref, ref, sem).wait()

    def send_query(array, portion, own):
        for target in range(last - 1, 0, -1):
            @pl.when(target < z)
            def _():
                array_copy(array, z, portion, target, own).start()

    def send_key(array, portion, own):
        @pl.when(up_key(z))
        def _():
            array_copy(array, z, portion, z + 1, own).start()

    for array in (QUERY, GRAD):
        send_query(array, x, True)
    @pl.when(down_key)
    def _():
        for array in (KEY, VALUE):
            array_copy(array, z, x, 0, True).start()
    @pl.when(z == 0)
    def _():
        for array in (KEY, VALUE, QUERY, GRAD):
            x_copy(array).start()
    @pl.when(z > 0)
    def _():
        for array in (QUERY, GRAD, KEY, VALUE):
            x_copy(array).start()
    x_ends().start()

    @pl.when(z < last)
    def _():
        pl.semaphore_wait(ready.at[z + 1], HEADS)
    for target in range(2, blocks):
        @pl.when(up_query & (target == z + 1))
        def _():
            for column in range(HEADS):
                up_ends(column).start()
            for column in (x, 1 - x):
                for array in (QUERY, GRAD):
                    query_copy(array, target, column).start()
    @pl.when(z == 0)
    def _():
        for array in (KEY, VALUE):
            send_key(array, x, True)

    def all_ready():
        @pl.loop(z + 2, blocks)
        def _(target):
            pl.semaphore_wait(ready.at[target], HEADS)

    def pass_on(array):
        landed(buf.at[array, z, other_rows], x_recv.at[array])
        if array in (KEY, VALUE):
            @pl.when(down_key)
            def _():
                array_copy(array, z, 1 - x, 0).start()
            @pl.when(prompt)
            def _():
                @pl.when(z > 0)
                def _():
                    send_key(array, x, True)
                send_key(array, 1 - x, False)
        else:
            send_query(array, 1 - x, False)

    def key_arrives(block):
        landed(buf.at[KEY:VALUE + 1, block], z_recv.at[0, block])
        @pl.when(up_key(block) & (block < z))
        def _():
            for array in (KEY, VALUE):
                for portion in range(HEADS):
                    array_copy(array, block, portion, z + 1).start()

    def query_arrives(block):
        landed(buf.at[QUERY:GRAD + 1, block], z_recv.at[1, block])

    def own_arrives():
        landed(buf.at[:, z, own_rows], local_sem.at[0])
        landed(ends.at[x], local_sem.at[1])
        landed(ends.at[1 - x], x_recv.at[4])

    def limits(block, slot):
        joined = jnp.concatenate([ends[slot + portion] for portion in range(HEADS)], axis=1)
        position = lax.broadcasted_iota(jnp.int32, (1, span), 1) + block * span
        return jnp.maximum(position + 1, joined)

    key_row = lax.broadcasted_iota(jnp.int32, (span, span), 0)

    def score(kind, slot, key_block, query_block, limit=None):
        scores = dot(buf[KEY, key_block], buf[QUERY, query_block], 1, 1) * scaling
        prob_grad = dot(buf[VALUE, key_block], buf[GRAD, query_block], 1, 1)
        if limit is not None:
            scores = jnp.where(key_row + key_block * span < limit, scores, HIDDEN)
        highest = jnp.max(scores, axis=0, keepdims=True)
        probs = jnp.exp(scores - highest)
        pe[kind, slot] = probs
        pd[kind, slot] = prob_grad
        pair_stats[kind, slot, 0:1] = highest
        pair_stats[kind, slot, 1:2] = jnp.sum(probs, axis=0, keepdims=True)
        pair_stats[kind, slot, 2:3] = jnp.sum(probs * prob_grad, axis=0, keepdims=True)

    def stat(ref):
        return ref[0:1], ref[1:2], ref[2:3]

    def pair_stat(kind, slot):
        return stat(pair_stats.at[kind, slot])

    def keep(ref, value):
        for row in range(3):
            ref[row:row + 1] = value[row]

    def merge(a, b):
        highest = jnp.maximum(a[0], b[0])
        fa, fb = jnp.exp(a[0] - highest), jnp.exp(b[0] - highest)
        return highest, a[1] * fa + b[1] * fb, a[2] * fa + b[2] * fb

    def stat_copy(block, target):
        return remote(st_out.at[block], st_in.at[z, block], st_recv.at[z - 1, block], target, x)

    def send_stat(block, value):
        keep(st_out.at[block], value)
        for target in range(1, blocks):
            @pl.when(takes_part(block, target) & (target != z))
            def _():
                stat_copy(block, target).start()

    def settle(block):
        keep(total, stat(st_out.at[block]))
        for source in range(1, blocks):
            @pl.when(takes_part(block, source) & (source != z))
            def _():
                landed(st_in.at[source, block], st_recv.at[source - 1, block])
                keep(total, merge(stat(total), stat(st_in.at[source, block])))
        finish(block, stat(total))

    def finish(block, value):
        fin[block, 0:1] = value[0] + jnp.log(value[1])
        fin[block, 1:2] = value[2] / value[1]

    def weights(kind, slot, block):
        probs = pe[kind, slot] * jnp.exp(pair_stats[kind, slot, 0:1] - fin[block, 0:1])
        score_grad = (probs * (pd[kind, slot] - fin[block, 1:2])).astype(jnp.bfloat16)
        return probs.astype(jnp.bfloat16), score_grad

    def ret_copy(slot, part, target, portion):
        return remote(
            ret_out.at[part, rows_of(portion)], ret_in.at[slot, x], ret_recv.at[slot], target, portion)

    def send_back(slot, part, target, value):
        ret_out[part] = (value * scaling if slot in (DQ, DK) else value).astype(jnp.bfloat16)
        for portion in range(HEADS):
            ret_copy(slot, part, target, portion).start()

    def res_copy(slot):
        return remote(res_out.at[slot], res_in.at[slot], res_recv.at[slot], z, 1 - x)

    def send_result(slot, acc):
        value = acc[other_rows, :]
        res_out[slot] = (value * scaling if slot in (DQ, DK) else value).astype(jnp.bfloat16)
        res_copy(slot).start()

    def emit(slot, returned):
        ref, acc = ((o_ref, acc_o), (dq_ref, acc_q), (dk_ref, acc_k), (dv_ref, acc_v))[slot]
        own = acc[own_rows, :]
        own = own * scaling if slot in (DQ, DK) else own
        res_copy(slot).wait_recv()
        other = res_in[slot].astype(jnp.float32)
        if returned:
            landed(ret_in.at[slot], ret_recv.at[slot])
            own = own + ret_in[slot, x].astype(jnp.float32)
            other = other + ret_in[slot, 1 - x].astype(jnp.float32)
        ref[:, own_columns] = own.astype(ref.dtype)
        ref[:, other_columns] = other.astype(ref.dtype)

    def key_side(kind, slot, block, into_v, into_k):
        probs, score_grad = weights(kind, slot, block)
        into_v[...] += dot(probs, buf[GRAD, block], 1, 0)
        into_k[...] += dot(score_grad, buf[QUERY, block], 1, 0)

    @pl.when(z == 0)
    def _():
        for array in (KEY, VALUE):
            pass_on(array)
        for array in (QUERY, GRAD):
            pass_on(array)
        own_arrives()
        limit = limits(0, 0)
        score(0, 0, 0, 0, limit)
        value = pair_stat(0, 0)
        if key_back:
            key_arrives(1)
            score(1, 0, 1, 0, limit)
            value = merge(value, pair_stat(1, 0))
        finish(0, value)
        probs, score_grad = weights(0, 0, 0)
        acc_o[...] = dot(probs, buf[VALUE, 0], 0, 0)
        acc_q[...] = dot(score_grad, buf[KEY, 0], 0, 0)
        acc_v[...] = dot(probs, buf[GRAD, 0], 1, 0)
        acc_k[...] = dot(score_grad, buf[QUERY, 0], 1, 0)
        if key_back:
            probs, score_grad = weights(1, 0, 0)
            send_back(DV, 0, 1, dot(probs, buf[GRAD, 0], 1, 0))
            send_back(DK, 1, 1, dot(score_grad, buf[QUERY, 0], 1, 0))
            acc_o[...] += dot(probs, buf[VALUE, 1], 0, 0)
            acc_q[...] += dot(score_grad, buf[KEY, 1], 0, 0)
        send_result(DV, acc_v)
        send_result(DK, acc_k)
        send_result(OUT, acc_o)
        send_result(DQ, acc_q)
        emit(OUT, False)
        emit(DQ, False)

    @pl.when(z == 1)
    def _():
        for array in (QUERY, GRAD, KEY, VALUE):
            pass_on(array)
        own_arrives()
        score(0, 1, 1, 1, limits(1, 0))
        @pl.when(jnp.logical_not(prompt))
        def _():
            for array in (KEY, VALUE):
                for portion in range(HEADS):
                    send_key(array, portion, False)
        key_arrives(0)
        score(1, 1, 0, 1)
        send_stat(1, merge(pair_stat(0, 1), pair_stat(1, 1)))
        all_ready()

        @pl.loop(2, blocks)
        def _(block):
            query_arrives(block)
            score(1, block, 0, block)
            score(0, block, 1, block)
            send_stat(block, merge(pair_stat(0, block), pair_stat(1, block)))

        alt[...] = jnp.zeros_like(alt)

        @pl.loop(2, last)
        def _(block):
            settle(block)
            key_side(1, block, block, alt.at[0], alt.at[1])

        settle(1)
        settle(last)
        near, near_grad = weights(1, 1, 1)
        far, far_grad = weights(1, last, last)
        ret_out[0] = (alt[0] + dot(near, buf[GRAD, 1], 1, 0) + dot(far, buf[GRAD, last], 1, 0)).astype(jnp.bfloat16)
        ret_copy(DV, 0, 0, 0).start()
        ret_out[1] = ((
            alt[1] + dot(near_grad, buf[QUERY, 1], 1, 0) + dot(far_grad, buf[QUERY, last], 1, 0)) * scaling
        ).astype(jnp.bfloat16)
        ret_copy(DK, 1, 0, 0).start()
        ret_copy(DV, 0, 0, 1).start()
        ret_copy(DK, 1, 0, 1).start()
        probs, score_grad = weights(0, last, last)
        send_back(OUT, 2, last, dot(far, buf[VALUE, 0], 0, 0) + dot(probs, buf[VALUE, 1], 0, 0))
        send_back(DQ, 3, last, dot(far_grad, buf[KEY, 0], 0, 0) + dot(score_grad, buf[KEY, 1], 0, 0))
        acc_v[...] = dot(probs, buf[GRAD, last], 1, 0)
        acc_k[...] = dot(score_grad, buf[QUERY, last], 1, 0)
        probs, score_grad = weights(0, 1, 1)
        acc_o[...] = dot(probs, buf[VALUE, 1], 0, 0) + dot(near, buf[VALUE, 0], 0, 0)
        send_result(OUT, acc_o)
        acc_q[...] = dot(score_grad, buf[KEY, 1], 0, 0) + dot(near_grad, buf[KEY, 0], 0, 0)
        send_result(DQ, acc_q)
        acc_v[...] += dot(probs, buf[GRAD, 1], 1, 0)
        acc_k[...] += dot(score_grad, buf[QUERY, 1], 1, 0)
        @pl.loop(2, last)
        def _(block):
            key_side(0, block, block, acc_v, acc_k)
        send_result(DV, acc_v)
        send_result(DK, acc_k)

    first_key = jnp.where(z == last, 2, 0)

    @pl.when(z >= 2)
    def _():
        for array in (QUERY, GRAD, KEY, VALUE):
            pass_on(array)
        own_arrives()
        score(0, z, z, z, limits(z, 0))
        send_stat(z, pair_stat(0, z))

        @pl.when(ahead(z - 1))
        def _():
            query_arrives(z - 1)
            landed(ends.at[HEADS:2 * HEADS], end_recv)
            score(0, z - 1, z, z - 1, limits(z - 1, HEADS))
            send_stat(z - 1, pair_stat(0, z - 1))

        @pl.loop(z + 1, blocks)
        def _(block):
            query_arrives(block)
            score(0, block, z, block)
            send_stat(block, pair_stat(0, block))

        all_ready()
        acc_k[...] = jnp.zeros_like(acc_k)
        acc_v[...] = jnp.zeros_like(acc_v)
        @pl.when(ahead(z - 1))
        def _():
            settle(z - 1)
            probs, score_grad = weights(0, z - 1, z - 1)
            send_back(OUT, 0, z - 1, dot(probs, buf[VALUE, z], 0, 0))
            send_back(DQ, 1, z - 1, dot(score_grad, buf[KEY, z], 0, 0))
            acc_v[...] += dot(probs, buf[GRAD, z - 1], 1, 0)
            acc_k[...] += dot(score_grad, buf[QUERY, z - 1], 1, 0)

        @pl.loop(1, z + 1 - first_key)
        def _(back):
            key_arrives(z - back)
            score(1, z - back, z - back, z)

        settle(z)
        probs, score_grad = weights(0, z, z)
        acc_o[...] = dot(probs, buf[VALUE, z], 0, 0)
        acc_q[...] = dot(score_grad, buf[KEY, z], 0, 0)
        acc_v[...] += dot(probs, buf[GRAD, z], 1, 0)
        acc_k[...] += dot(score_grad, buf[QUERY, z], 1, 0)

        @pl.loop(1, z + 1 - first_key)
        def _(back):
            block = z - back
            probs, score_grad = weights(1, block, z)
            acc_o[...] += dot(probs, buf[VALUE, block], 0, 0)
            acc_q[...] += dot(score_grad, buf[KEY, block], 0, 0)
        send_result(OUT, acc_o)
        send_result(DQ, acc_q)

        @pl.loop(z + 1, blocks)
        def _(block):
            settle(block)
            key_side(0, block, block, acc_v, acc_k)
        send_result(DV, acc_v)
        send_result(DK, acc_k)

    @pl.when(z == 0)
    def _():
        all_ready()
    for _ in range(4):
        res_copy(0).wait_send()
        x_copy(0).wait_send()
    x_ends().wait_send()
    @pl.when(up_query)
    def _():
        for column in range(HEADS):
            up_ends(column).wait_send()
            for array in (QUERY, GRAD):
                query_copy(array, z + 1, column).wait_send()
    @pl.loop(1, z)
    def _(target):
        for _ in range(4):
            array_copy(QUERY, z, 0, target).wait_send()
    @pl.when(down_key)
    def _():
        for _ in range(4):
            array_copy(KEY, z, 0, 0).wait_send()
    @pl.loop(0, z + 1)
    def _(block):
        @pl.when(up_key(block))
        def _():
            for _ in range(4):
                array_copy(KEY, block, 0, z + 1).wait_send()
    @pl.when(z >= 1)
    def _():
        @pl.loop(jnp.maximum(z - 1, 1), blocks)
        def _(block):
            @pl.when((block >= z) | ahead(z - 1))
            def _():
                for target in range(1, blocks):
                    @pl.when(takes_part(block, target) & (target != z))
                    def _():
                        stat_copy(block, target).wait_send()
    for part, wanted in ((0, ((z == 0) & ahead(0)) | (z == 1) | ((z >= 2) & ahead(z - 1))), (2, z == 1)):
        @pl.when(wanted)
        def _():
            for _ in range(4):
                ret_copy(0, part, 0, 0).wait_send()

    @pl.when(z == 0)
    def _():
        emit(DV, True)
        emit(DK, True)
    @pl.when(z == 1)
    def _():
        emit(OUT, query_back)
        emit(DQ, query_back)
        emit(DV, key_back)
        emit(DK, key_back)
    @pl.when(z >= 2)
    def _():
        returned = ahead(z) | (z == last)
        @pl.when(returned)
        def _():
            emit(OUT, True)
            emit(DQ, True)
        @pl.when(jnp.logical_not(returned))
        def _():
            emit(OUT, False)
            emit(DQ, False)
        emit(DV, False)
        emit(DK, False)


def flush(*refs):
    sem = refs[-1]
    copies = [pltpu.make_async_copy(refs[i], refs[i + 4], sem.at[i]) for i in range(4)]
    for copy in copies:
        copy.start()
    for copy in copies:
        copy.wait()


def solution(mesh):
    n = mesh.shape["ctx"]

    def local(queries, keys, values, out_grad, span_end):
        rows = queries.shape[0]
        blocks, span = n // HEADS, HEADS * rows
        f32, bf16 = jnp.float32, jnp.bfloat16
        anywhere = pl.BlockSpec(memory_space=pl.ANY)
        vmem = pl.BlockSpec(memory_space=pltpu.VMEM)
        dma = pltpu.SemaphoreType.DMA
        results = pl.pallas_call(
            functools.partial(kernel, n, rows),
            out_shape=tuple(
                pltpu.VMEM(queries.shape, kind) for kind in (bf16, f32, f32, f32)),
            in_specs=[anywhere] * 5,
            out_specs=(vmem,) * 4,
            scratch_shapes=[
                pltpu.VMEM((4, blocks, span, HEAD_DIM), bf16),
                pltpu.VMEM((2 * HEADS, 1, rows), jnp.int32),
                pltpu.VMEM((2, blocks, span, span), f32),
                pltpu.VMEM((2, blocks, span, span), f32),
                pltpu.VMEM((2, blocks, 3, span), f32),
                pltpu.VMEM((blocks, blocks, 3, span), f32),
                pltpu.VMEM((blocks, 3, span), f32),
                pltpu.VMEM((3, span), f32),
                pltpu.VMEM((blocks, 2, span), f32),
                pltpu.VMEM((span, HEAD_DIM), f32),
                pltpu.VMEM((span, HEAD_DIM), f32),
                pltpu.VMEM((span, HEAD_DIM), f32),
                pltpu.VMEM((span, HEAD_DIM), f32),
                pltpu.VMEM((2, span, HEAD_DIM), f32),
                pltpu.VMEM((4, span, HEAD_DIM), bf16),
                pltpu.VMEM((4, HEADS, rows, HEAD_DIM), bf16),
                pltpu.VMEM((4, rows, HEAD_DIM), bf16),
                pltpu.VMEM((4, rows, HEAD_DIM), bf16),
                dma((2,)),
                dma((5,)),
                dma((2, blocks)),
                dma,
                dma((blocks - 1, blocks)),
                dma((4,)),
                dma((4,)),
                dma,
                pltpu.SemaphoreType.REGULAR((blocks,)),
            ],
            compiler_params=pltpu.CompilerParams(collective_id=0, has_side_effects=True),
        )(queries, keys, values, out_grad, span_end[None])
        return pl.pallas_call(
            flush,
            out_shape=tuple(
                jax.ShapeDtypeStruct(queries.shape, kind) for kind in (bf16, f32, f32, f32)),
            in_specs=[vmem] * 4,
            out_specs=(anywhere,) * 4,
            scratch_shapes=[dma((4,))],
        )(*(pltpu.with_memory_space_constraint(result, pltpu.VMEM) for result in results))

    spec = P(("dp", "ctx"), None)
    return jax.shard_map(
        local, mesh=mesh, in_specs=(spec,) * 4 + (P(("dp", "ctx")),),
        out_specs=(spec,) * 4, check_vma=False)
```

```python
import functools

import jax
import jax.numpy as jnp
from jax import lax
from jax.experimental import pallas as pl
from jax.experimental.pallas import tpu as pltpu
from jax.sharding import PartitionSpec as P

HEADS = 2
HEAD_DIM = 128
IMG = 288
HIDDEN = -1e30
KEY, VALUE, QUERY, GRAD = range(4)


def dot(a, b, a_dim, b_dim):
    return lax.dot_general(a, b, (((a_dim,), (b_dim,)), ((), ())), preferred_element_type=jnp.float32)


def kernel(
    n, rows,
    q_in, k_in, v_in, g_in, ends_in,
    o_ref, dq_ref, dk_ref, dv_ref,
    buf, ends, pe, pd, pair_stats, st_in, st_out, total, fin,
    acc_o, acc_q, acc_k, acc_v, alt, ret_out, ret_in, res_out, res_in,
    local_sem, x_recv, z_recv, end_recv, st_recv, ret_recv, res_recv, sent, ready,
):
    scaling = HEAD_DIM ** -0.5
    blocks = n // HEADS
    span = HEADS * rows
    cut = blocks * span - IMG
    last = blocks - 1
    me = lax.axis_index("ctx")
    z = me // HEADS
    x = me % HEADS
    sources = (k_in, v_in, q_in, g_in)
    OUT, DQ, DK, DV = range(4)

    def device(block, column):
        return {"ctx": block * HEADS + column}

    def ahead(block):
        return ((block + 1) * span < cut) & (block + 1 < blocks)

    def rows_of(portion):
        return pl.ds(pl.multiple_of(portion * rows, 16), rows)

    def columns_of(head):
        return pl.ds(pl.multiple_of(head * HEAD_DIM, HEAD_DIM), HEAD_DIM)

    own_rows, other_rows = rows_of(x), rows_of(1 - x)
    own_columns, other_columns = columns_of(x), columns_of(1 - x)

    key_back = span < cut
    query_back = 2 * span < cut and last > 1
    down_key = (z == 1) & ahead(0)
    up_query = (z >= 1) & ahead(z)

    def up_key(block):
        return (z < last) & ((z == 0) | (block >= 2))

    def takes_part(block, target):
        return (target >= 1) & ((target <= block) | ((target == block + 1) & ahead(block)))

    barrier = pltpu.get_barrier_semaphore()
    for target in range(1, blocks):
        @pl.when(target > z)
        def _():
            for column in range(HEADS):
                pl.semaphore_signal(barrier, inc=1, device_id=device(target, column))
    pl.semaphore_signal(barrier, inc=1, device_id=device(z, 1 - x))

    def own_copy(array):
        return pltpu.make_async_copy(
            sources[array].at[:, own_columns], buf.at[array, z, own_rows], local_sem.at[0])

    for array in range(4):
        own_copy(array).start()
    pltpu.make_async_copy(ends_in, ends.at[x], local_sem.at[1]).start()

    pl.semaphore_wait(barrier, HEADS * z + 1)
    for target in range(last):
        @pl.when(target < z)
        def _():
            for column in range(HEADS):
                pl.semaphore_signal(ready.at[z], inc=1, device_id=device(target, column))

    def remote(src, dst, recv, target, column):
        return pltpu.make_async_remote_copy(
            src_ref=src, dst_ref=dst, send_sem=sent, recv_sem=recv, device_id=device(target, column))

    def array_copy(array, block, portion, target, own=False):
        dst = buf.at[array, block, rows_of(portion)]
        return remote(
            sources[array].at[:, own_columns] if own else dst, dst,
            z_recv.at[array // 2, block], target, x)

    def query_copy(array, target, column):
        return remote(
            sources[array].at[:, columns_of(column)], buf.at[array, z, own_rows],
            z_recv.at[array // 2, z], target, column)

    def x_copy(array):
        return remote(
            sources[array].at[:, other_columns], buf.at[array, z, own_rows], x_recv.at[array], z, 1 - x)

    def x_ends():
        return remote(ends_in, ends.at[x], x_recv.at[4], z, 1 - x)

    def up_ends(column):
        return remote(ends_in, ends.at[HEADS + x], end_recv, z + 1, column)

    def landed(ref, sem):
        pltpu.make_async_copy(ref, ref, sem).wait()

    def send_query(target):
        for column in (x, 1 - x):
            for array in (QUERY, GRAD):
                query_copy(array, target, column).start()

    def send_key(array, portion, own):
        @pl.when(up_key(z))
        def _():
            array_copy(array, z, portion, z + 1, own).start()

    for target in range(last - 1, 0, -1):
        @pl.when((target < z) & (z > 2))
        def _():
            for array in (QUERY, GRAD):
                query_copy(array, target, x).start()
    @pl.when(z == 2)
    def _():
        send_query(1)
    @pl.when(down_key)
    def _():
        for column in (x, 1 - x):
            for array in (KEY, VALUE):
                query_copy(array, 0, column).start()
    @pl.when(z == 0)
    def _():
        for array in (KEY, VALUE, QUERY, GRAD):
            x_copy(array).start()
    @pl.when(z > 0)
    def _():
        for array in (QUERY, GRAD, KEY, VALUE):
            x_copy(array).start()
    x_ends().start()

    @pl.when(z < last)
    def _():
        pl.semaphore_wait(ready.at[z + 1], HEADS)
    for target in range(2, blocks):
        @pl.when(up_query & (target == z + 1))
        def _():
            for column in range(HEADS):
                up_ends(column).start()
            send_query(target)
    @pl.when(z == 0)
    def _():
        for array in (KEY, VALUE):
            send_key(array, x, True)

    def all_ready():
        @pl.loop(z + 2, blocks)
        def _(target):
            pl.semaphore_wait(ready.at[target], HEADS)

    def pass_on(array):
        landed(buf.at[array, z, other_rows], x_recv.at[array])
        if array in (KEY, VALUE):
            @pl.when(z > 0)
            def _():
                send_key(array, x, True)
            send_key(array, 1 - x, False)
        elif array == GRAD:
            for target in range(last - 1, 0, -1):
                @pl.when((target < z) & (z > 2))
                def _():
                    for half in (QUERY, GRAD):
                        array_copy(half, z, 1 - x, target).start()

    def key_arrives(block):
        landed(buf.at[KEY:VALUE + 1, block], z_recv.at[0, block])
        @pl.when(up_key(block) & (block < z))
        def _():
            for array in (KEY, VALUE):
                for portion in range(HEADS):
                    array_copy(array, block, portion, z + 1).start()

    def query_arrives(block):
        landed(buf.at[QUERY:GRAD + 1, block], z_recv.at[1, block])

    def own_arrives():
        landed(buf.at[:, z, own_rows], local_sem.at[0])
        landed(ends.at[x], local_sem.at[1])
        landed(ends.at[1 - x], x_recv.at[4])

    def limits(block, slot):
        joined = jnp.concatenate([ends[slot + portion] for portion in range(HEADS)], axis=1)
        position = lax.broadcasted_iota(jnp.int32, (1, span), 1) + block * span
        return jnp.maximum(position + 1, joined)

    key_row = lax.broadcasted_iota(jnp.int32, (span, span), 0)

    def score(kind, slot, key_block, query_block, limit=None):
        scores = dot(buf[KEY, key_block], buf[QUERY, query_block], 1, 1) * scaling
        prob_grad = dot(buf[VALUE, key_block], buf[GRAD, query_block], 1, 1)
        if limit is not None:
            scores = jnp.where(key_row + key_block * span < limit, scores, HIDDEN)
        highest = jnp.max(scores, axis=0, keepdims=True)
        probs = jnp.exp(scores - highest)
        pe[kind, slot] = probs
        pd[kind, slot] = prob_grad
        pair_stats[kind, slot, 0:1] = highest
        pair_stats[kind, slot, 1:2] = jnp.sum(probs, axis=0, keepdims=True)
        pair_stats[kind, slot, 2:3] = jnp.sum(probs * prob_grad, axis=0, keepdims=True)

    def stat(ref):
        return ref[0:1], ref[1:2], ref[2:3]

    def pair_stat(kind, slot):
        return stat(pair_stats.at[kind, slot])

    def keep(ref, value):
        for row in range(3):
            ref[row:row + 1] = value[row]

    def merge(a, b):
        highest = jnp.maximum(a[0], b[0])
        fa, fb = jnp.exp(a[0] - highest), jnp.exp(b[0] - highest)
        return highest, a[1] * fa + b[1] * fb, a[2] * fa + b[2] * fb

    def stat_copy(block, target):
        return remote(st_out.at[block], st_in.at[z, block], st_recv.at[z - 1, block], target, x)

    def send_stat(block, value):
        keep(st_out.at[block], value)
        for target in range(1, blocks):
            @pl.when(takes_part(block, target) & (target != z))
            def _():
                stat_copy(block, target).start()

    def settle(block):
        keep(total, stat(st_out.at[block]))
        for source in range(1, blocks):
            @pl.when(takes_part(block, source) & (source != z))
            def _():
                landed(st_in.at[source, block], st_recv.at[source - 1, block])
                keep(total, merge(stat(total), stat(st_in.at[source, block])))
        finish(block, stat(total))

    def finish(block, value):
        fin[block, 0:1] = value[0] + jnp.log(value[1])
        fin[block, 1:2] = value[2] / value[1]

    def weights(kind, slot, block):
        probs = pe[kind, slot] * jnp.exp(pair_stats[kind, slot, 0:1] - fin[block, 0:1])
        score_grad = (probs * (pd[kind, slot] - fin[block, 1:2])).astype(jnp.bfloat16)
        return probs.astype(jnp.bfloat16), score_grad

    def ret_copy(origin, slot, part, target, portion):
        return remote(
            ret_out.at[part, rows_of(portion)], ret_in.at[origin, slot, x], ret_recv.at[origin, slot],
            target, portion)

    def send_back(origin, slot, part, target, value):
        ret_out[part] = (value * scaling if slot in (DQ, DK) else value).astype(jnp.bfloat16)
        for portion in range(HEADS):
            ret_copy(origin, slot, part, target, portion).start()

    def res_copy(slot):
        return remote(res_out.at[slot], res_in.at[slot], res_recv.at[slot], z, 1 - x)

    def send_result(slot, acc):
        value = acc[other_rows, :]
        res_out[slot] = (value * scaling if slot in (DQ, DK) else value).astype(jnp.bfloat16)
        res_copy(slot).start()

    HUB, SIDE = range(2)

    def emit(slot, *origins):
        ref, acc = ((o_ref, acc_o), (dq_ref, acc_q), (dk_ref, acc_k), (dv_ref, acc_v))[slot]
        own = acc[own_rows, :]
        own = own * scaling if slot in (DQ, DK) else own
        res_copy(slot).wait_recv()
        other = res_in[slot].astype(jnp.float32)
        for origin in origins:
            landed(ret_in.at[origin, slot], ret_recv.at[origin, slot])
            own = own + ret_in[origin, slot, x].astype(jnp.float32)
            other = other + ret_in[origin, slot, 1 - x].astype(jnp.float32)
        ref[:, own_columns] = own.astype(ref.dtype)
        ref[:, other_columns] = other.astype(ref.dtype)

    def key_side(kind, slot, block, into_v, into_k):
        probs, score_grad = weights(kind, slot, block)
        into_v[...] += dot(probs, buf[GRAD, block], 1, 0)
        into_k[...] += dot(score_grad, buf[QUERY, block], 1, 0)

    @pl.when(z == 0)
    def _():
        for array in (KEY, VALUE):
            pass_on(array)
        for array in (QUERY, GRAD):
            pass_on(array)
        own_arrives()
        limit = limits(0, 0)
        score(0, 0, 0, 0, limit)
        value = pair_stat(0, 0)
        if key_back:
            key_arrives(1)
            score(1, 0, 1, 0, limit)
            value = merge(value, pair_stat(1, 0))
        finish(0, value)
        probs, score_grad = weights(0, 0, 0)
        acc_o[...] = dot(probs, buf[VALUE, 0], 0, 0)
        acc_q[...] = dot(score_grad, buf[KEY, 0], 0, 0)
        acc_v[...] = dot(probs, buf[GRAD, 0], 1, 0)
        acc_k[...] = dot(score_grad, buf[QUERY, 0], 1, 0)
        if key_back:
            probs, score_grad = weights(1, 0, 0)
            send_back(SIDE, DV, 0, 1, dot(probs, buf[GRAD, 0], 1, 0))
            send_back(SIDE, DK, 1, 1, dot(score_grad, buf[QUERY, 0], 1, 0))
            acc_o[...] += dot(probs, buf[VALUE, 1], 0, 0)
            acc_q[...] += dot(score_grad, buf[KEY, 1], 0, 0)
        send_result(DV, acc_v)
        send_result(DK, acc_k)
        send_result(OUT, acc_o)
        send_result(DQ, acc_q)
        emit(OUT)
        emit(DQ)

    @pl.when(z == 1)
    def _():
        for array in (QUERY, GRAD, KEY, VALUE):
            pass_on(array)
        own_arrives()
        score(0, 1, 1, 1, limits(1, 0))
        key_arrives(0)
        score(1, 1, 0, 1)
        send_stat(1, merge(pair_stat(0, 1), pair_stat(1, 1)))
        all_ready()

        def scores_of(block):
            query_arrives(block)
            score(1, block, 0, block)
            score(0, block, 1, block)
            send_stat(block, merge(pair_stat(0, block), pair_stat(1, block)))

        def query_side(far, far_grad, near, near_grad):
            return (
                dot(far, buf[VALUE, 0], 0, 0) + dot(near, buf[VALUE, 1], 0, 0),
                dot(far_grad, buf[KEY, 0], 0, 0) + dot(near_grad, buf[KEY, 1], 0, 0))

        alt[...] = jnp.zeros_like(alt)

        @pl.loop(2, blocks)
        def _(block):
            scores_of(block)

        @pl.loop(2, last)
        def _(block):
            settle(block)
            key_side(1, block, block, alt.at[0], alt.at[1])
        settle(1)
        key_side(1, 1, 1, alt.at[0], alt.at[1])
        settle(last)
        far, far_grad = weights(1, last, last)
        ret_out[0] = (alt[0] + dot(far, buf[GRAD, last], 1, 0)).astype(jnp.bfloat16)
        ret_copy(HUB, DV, 0, 0, 0).start()
        ret_out[1] = ((alt[1] + dot(far_grad, buf[QUERY, last], 1, 0)) * scaling).astype(jnp.bfloat16)
        ret_copy(HUB, DK, 1, 0, 0).start()
        ret_copy(HUB, DV, 0, 0, 1).start()
        ret_copy(HUB, DK, 1, 0, 1).start()
        near, near_grad = weights(0, last, last)
        output, query_grad = query_side(far, far_grad, near, near_grad)
        send_back(HUB, OUT, 2 * last, last, output)
        send_back(HUB, DQ, 2 * last + 1, last, query_grad)
        acc_v[...] = dot(near, buf[GRAD, last], 1, 0)
        acc_k[...] = dot(near_grad, buf[QUERY, last], 1, 0)

        far, far_grad = weights(1, 1, 1)
        near, near_grad = weights(0, 1, 1)
        acc_o[...], acc_q[...] = query_side(far, far_grad, near, near_grad)
        send_result(OUT, acc_o)
        send_result(DQ, acc_q)
        acc_v[...] += dot(near, buf[GRAD, 1], 1, 0)
        acc_k[...] += dot(near_grad, buf[QUERY, 1], 1, 0)

        @pl.loop(2, last)
        def _(block):
            far, far_grad = weights(1, block, block)
            near, near_grad = weights(0, block, block)
            acc_v[...] += dot(near, buf[GRAD, block], 1, 0)
            acc_k[...] += dot(near_grad, buf[QUERY, block], 1, 0)
            output, query_grad = query_side(far, far_grad, near, near_grad)
            send_back(HUB, OUT, 2 * block, block, output)
            send_back(HUB, DQ, 2 * block + 1, block, query_grad)
        send_result(DV, acc_v)
        send_result(DK, acc_k)

    @pl.when(z >= 2)
    def _():
        for array in (QUERY, GRAD, KEY, VALUE):
            pass_on(array)
        own_arrives()
        score(0, z, z, z, limits(z, 0))
        send_stat(z, pair_stat(0, z))

        @pl.when(ahead(z - 1))
        def _():
            query_arrives(z - 1)
            landed(ends.at[HEADS:2 * HEADS], end_recv)
            score(0, z - 1, z, z - 1, limits(z - 1, HEADS))
            send_stat(z - 1, pair_stat(0, z - 1))

        @pl.loop(z + 1, blocks)
        def _(block):
            query_arrives(block)
            score(0, block, z, block)
            send_stat(block, pair_stat(0, block))

        all_ready()
        acc_k[...] = jnp.zeros_like(acc_k)
        acc_v[...] = jnp.zeros_like(acc_v)
        @pl.when(ahead(z - 1))
        def _():
            settle(z - 1)
            probs, score_grad = weights(0, z - 1, z - 1)
            send_back(SIDE, OUT, 0, z - 1, dot(probs, buf[VALUE, z], 0, 0))
            send_back(SIDE, DQ, 1, z - 1, dot(score_grad, buf[KEY, z], 0, 0))
            acc_v[...] += dot(probs, buf[GRAD, z - 1], 1, 0)
            acc_k[...] += dot(score_grad, buf[QUERY, z - 1], 1, 0)

        @pl.loop(1, z - 1)
        def _(back):
            key_arrives(z - back)
            score(1, z - back, z - back, z)

        settle(z)
        probs, score_grad = weights(0, z, z)
        acc_v[...] += dot(probs, buf[GRAD, z], 1, 0)
        acc_k[...] += dot(score_grad, buf[QUERY, z], 1, 0)
        @pl.when(z == last)
        def _():
            send_result(DV, acc_v)
            send_result(DK, acc_k)
        acc_o[...] = dot(probs, buf[VALUE, z], 0, 0)
        acc_q[...] = dot(score_grad, buf[KEY, z], 0, 0)

        @pl.loop(1, z - 1)
        def _(back):
            block = z - back
            probs, score_grad = weights(1, block, z)
            acc_o[...] += dot(probs, buf[VALUE, block], 0, 0)
            acc_q[...] += dot(score_grad, buf[KEY, block], 0, 0)
        send_result(OUT, acc_o)
        send_result(DQ, acc_q)

        @pl.when(z < last)
        def _():
            @pl.loop(z + 1, blocks)
            def _(block):
                settle(block)
                key_side(0, block, block, acc_v, acc_k)
            send_result(DV, acc_v)
            send_result(DK, acc_k)

    @pl.when(z == 0)
    def _():
        all_ready()
    for _ in range(4):
        res_copy(0).wait_send()
        x_copy(0).wait_send()
    x_ends().wait_send()
    @pl.when(up_query)
    def _():
        for column in range(HEADS):
            up_ends(column).wait_send()
            for array in (QUERY, GRAD):
                query_copy(array, z + 1, column).wait_send()
    @pl.loop(1, z)
    def _(target):
        for _ in range(4):
            query_copy(QUERY, target, x).wait_send()
    @pl.when(down_key)
    def _():
        for _ in range(4):
            query_copy(KEY, 0, x).wait_send()
    @pl.loop(0, z + 1)
    def _(block):
        @pl.when(up_key(block))
        def _():
            for _ in range(4):
                array_copy(KEY, block, 0, z + 1).wait_send()
    @pl.when(z >= 1)
    def _():
        @pl.loop(jnp.maximum(z - 1, 1), blocks)
        def _(block):
            @pl.when((block >= z) | ahead(z - 1))
            def _():
                for target in range(1, blocks):
                    @pl.when(takes_part(block, target) & (target != z))
                    def _():
                        stat_copy(block, target).wait_send()
    @pl.when(((z == 0) & ahead(0)) | (z == 1) | ((z >= 2) & ahead(z - 1)))
    def _():
        for _ in range(4):
            ret_copy(HUB, OUT, 0, 0, 0).wait_send()
    @pl.when(z == 1)
    def _():
        @pl.loop(2, blocks)
        def _(block):
            for _ in range(4):
                ret_copy(HUB, OUT, 0, 0, 0).wait_send()

    @pl.when(z == 0)
    def _():
        emit(DV, HUB)
        emit(DK, HUB)
    @pl.when(z == 1)
    def _():
        for slot in (OUT, DQ):
            emit(slot, *((SIDE,) if query_back else ()))
        for slot in (DV, DK):
            emit(slot, *((SIDE,) if key_back else ()))
    @pl.when(z >= 2)
    def _():
        @pl.when(ahead(z))
        def _():
            emit(OUT, HUB, SIDE)
            emit(DQ, HUB, SIDE)
        @pl.when(jnp.logical_not(ahead(z)))
        def _():
            emit(OUT, HUB)
            emit(DQ, HUB)
        emit(DV)
        emit(DK)


def flush(*refs):
    sem = refs[-1]
    copies = [pltpu.make_async_copy(refs[i], refs[i + 4], sem.at[i]) for i in range(4)]
    for copy in copies:
        copy.start()
    for copy in copies:
        copy.wait()


def solution(mesh):
    n = mesh.shape["ctx"]

    def local(queries, keys, values, out_grad, span_end):
        rows = queries.shape[0]
        blocks, span = n // HEADS, HEADS * rows
        f32, bf16 = jnp.float32, jnp.bfloat16
        anywhere = pl.BlockSpec(memory_space=pl.ANY)
        vmem = pl.BlockSpec(memory_space=pltpu.VMEM)
        dma = pltpu.SemaphoreType.DMA
        results = pl.pallas_call(
            functools.partial(kernel, n, rows),
            out_shape=tuple(
                pltpu.VMEM(queries.shape, kind) for kind in (bf16, f32, f32, f32)),
            in_specs=[anywhere] * 5,
            out_specs=(vmem,) * 4,
            scratch_shapes=[
                pltpu.VMEM((4, blocks, span, HEAD_DIM), bf16),
                pltpu.VMEM((2 * HEADS, 1, rows), jnp.int32),
                pltpu.VMEM((2, blocks, span, span), f32),
                pltpu.VMEM((2, blocks, span, span), f32),
                pltpu.VMEM((2, blocks, 3, span), f32),
                pltpu.VMEM((blocks, blocks, 3, span), f32),
                pltpu.VMEM((blocks, 3, span), f32),
                pltpu.VMEM((3, span), f32),
                pltpu.VMEM((blocks, 2, span), f32),
                pltpu.VMEM((span, HEAD_DIM), f32),
                pltpu.VMEM((span, HEAD_DIM), f32),
                pltpu.VMEM((span, HEAD_DIM), f32),
                pltpu.VMEM((span, HEAD_DIM), f32),
                pltpu.VMEM((2, span, HEAD_DIM), f32),
                pltpu.VMEM((2 * blocks, span, HEAD_DIM), bf16),
                pltpu.VMEM((2, 4, HEADS, rows, HEAD_DIM), bf16),
                pltpu.VMEM((4, rows, HEAD_DIM), bf16),
                pltpu.VMEM((4, rows, HEAD_DIM), bf16),
                dma((2,)),
                dma((5,)),
                dma((2, blocks)),
                dma,
                dma((blocks - 1, blocks)),
                dma((2, 4)),
                dma((4,)),
                dma,
                pltpu.SemaphoreType.REGULAR((blocks,)),
            ],
            compiler_params=pltpu.CompilerParams(collective_id=0, has_side_effects=True),
        )(queries, keys, values, out_grad, span_end[None])
        return pl.pallas_call(
            flush,
            out_shape=tuple(
                jax.ShapeDtypeStruct(queries.shape, kind) for kind in (bf16, f32, f32, f32)),
            in_specs=[vmem] * 4,
            out_specs=(anywhere,) * 4,
            scratch_shapes=[dma((4,))],
        )(*(pltpu.with_memory_space_constraint(result, pltpu.VMEM) for result in results))

    spec = P(("dp", "ctx"), None)
    return jax.shard_map(
        local, mesh=mesh, in_specs=(spec,) * 4 + (P(("dp", "ctx")),),
        out_specs=(spec,) * 4, check_vma=False)
```

```python
import functools

import jax
import jax.numpy as jnp
from jax import lax
from jax.experimental import pallas as pl
from jax.experimental.pallas import tpu as pltpu
from jax.sharding import PartitionSpec as P

HEADS = 2
HEAD_DIM = 128
IMG = 288
HIDDEN = -1e30
KEY, VALUE, QUERY, GRAD = range(4)


def dot(a, b, a_dim, b_dim):
    return lax.dot_general(a, b, (((a_dim,), (b_dim,)), ((), ())), preferred_element_type=jnp.float32)


def kernel(
    n, rows,
    q_in, k_in, v_in, g_in, ends_in,
    o_ref, dq_ref, dk_ref, dv_ref,
    buf, ends, pe, pd, pair_stats, st_in, st_out, total, fin,
    acc_o, acc_q, acc_k, acc_v, alt, ret_out, ret_in, res_out, res_in,
    local_sem, x_recv, z_recv, end_recv, st_recv, ret_recv, res_recv, sent, ready,
):
    scaling = HEAD_DIM ** -0.5
    blocks = n // HEADS
    span = HEADS * rows
    cut = blocks * span - IMG
    last = blocks - 1
    me = lax.axis_index("ctx")
    z = me // HEADS
    x = me % HEADS
    sources = (k_in, v_in, q_in, g_in)
    OUT, DQ, DK, DV = range(4)

    def device(block, column):
        return {"ctx": block * HEADS + column}

    def ahead(block):
        return ((block + 1) * span < cut) & (block + 1 < blocks)

    def rows_of(portion):
        return pl.ds(pl.multiple_of(portion * rows, 16), rows)

    def columns_of(head):
        return pl.ds(pl.multiple_of(head * HEAD_DIM, HEAD_DIM), HEAD_DIM)

    own_rows, other_rows = rows_of(x), rows_of(1 - x)
    own_columns, other_columns = columns_of(x), columns_of(1 - x)

    key_back = span < cut
    query_back = 2 * span < cut and last > 1
    down_key = (z == 1) & ahead(0)
    up_query = (z >= 1) & ahead(z)

    def up_key(block):
        return (z < last) & ((z == 0) | (block >= 2))

    def takes_part(block, target):
        return (target >= 1) & ((target <= block) | ((target == block + 1) & ahead(block)))

    barrier = pltpu.get_barrier_semaphore()
    for target in range(1, blocks):
        @pl.when(target > z)
        def _():
            for column in range(HEADS):
                pl.semaphore_signal(barrier, inc=1, device_id=device(target, column))
    pl.semaphore_signal(barrier, inc=1, device_id=device(z, 1 - x))

    def own_copy(array):
        return pltpu.make_async_copy(
            sources[array].at[:, own_columns], buf.at[array, z, own_rows], local_sem.at[0])

    for array in range(4):
        own_copy(array).start()
    pltpu.make_async_copy(ends_in, ends.at[x], local_sem.at[1]).start()

    pl.semaphore_wait(barrier, HEADS * z + 1)
    for target in range(last):
        @pl.when(target < z)
        def _():
            for column in range(HEADS):
                pl.semaphore_signal(ready.at[z - 1], inc=1, device_id=device(target, column))

    def remote(src, dst, recv, target, column):
        return pltpu.make_async_remote_copy(
            src_ref=src, dst_ref=dst, send_sem=sent, recv_sem=recv, device_id=device(target, column))

    def array_copy(array, block, portion, target, own=False):
        dst = buf.at[array, block, rows_of(portion)]
        return remote(
            sources[array].at[:, own_columns] if own else dst, dst,
            z_recv.at[array // 2, block], target, x)

    def query_copy(array, target, column):
        return remote(
            sources[array].at[:, columns_of(column)], buf.at[array, z, own_rows],
            z_recv.at[array // 2, z], target, column)

    def x_copy(array):
        return remote(
            sources[array].at[:, other_columns], buf.at[array, z, own_rows], x_recv.at[array], z, 1 - x)

    def x_ends():
        return remote(ends_in, ends.at[x], x_recv.at[4], z, 1 - x)

    def up_ends(column):
        return remote(ends_in, ends.at[HEADS + x], end_recv, z + 1, column)

    def landed(ref, sem):
        pltpu.make_async_copy(ref, ref, sem).wait()

    def send_query(target):
        for column in (x, 1 - x):
            for array in (QUERY, GRAD):
                query_copy(array, target, column).start()

    def send_key(array, portion, own):
        @pl.when(up_key(z))
        def _():
            array_copy(array, z, portion, z + 1, own).start()

    @pl.when(z == 0)
    def _():
        for array in (KEY, VALUE, QUERY, GRAD):
            x_copy(array).start()
    @pl.when(z > 0)
    def _():
        for array in (QUERY, GRAD, KEY, VALUE):
            x_copy(array).start()
    for target in range(last - 1, 0, -1):
        @pl.when((target < z) & (z > 2))
        def _():
            for array in (QUERY, GRAD):
                query_copy(array, target, x).start()
    @pl.when(z == 2)
    def _():
        send_query(1)
    @pl.when(down_key)
    def _():
        for column in (x, 1 - x):
            for array in (KEY, VALUE):
                query_copy(array, 0, column).start()
    x_ends().start()

    @pl.when(z < last)
    def _():
        pl.semaphore_wait(ready.at[z], HEADS)
    for target in range(2, blocks):
        @pl.when(up_query & (target == z + 1))
        def _():
            for column in range(HEADS):
                up_ends(column).start()
            send_query(target)
    @pl.when(z == 0)
    def _():
        for array in (KEY, VALUE):
            send_key(array, x, True)

    def all_ready():
        @pl.loop(z + 2, blocks)
        def _(target):
            pl.semaphore_wait(ready.at[target - 1], HEADS)

    def pass_on(array):
        landed(buf.at[array, z, other_rows], x_recv.at[array])
        if array in (KEY, VALUE):
            @pl.when(z > 0)
            def _():
                send_key(array, x, True)
            send_key(array, 1 - x, False)
        else:
            @pl.when(z > 2)
            def _():
                array_copy(array, z, 1 - x, z - 1).start()
                if array == GRAD:
                    for target in range(last - 2, 0, -1):
                        @pl.when(target < z - 1)
                        def _():
                            for half in (QUERY, GRAD):
                                array_copy(half, z, 1 - x, target).start()

    def key_arrives(block):
        landed(buf.at[KEY:VALUE + 1, block], z_recv.at[0, block])
        @pl.when(up_key(block) & (block < z))
        def _():
            for array in (KEY, VALUE):
                for portion in range(HEADS):
                    array_copy(array, block, portion, z + 1).start()

    def query_arrives(block):
        landed(buf.at[QUERY:GRAD + 1, block], z_recv.at[1, block])

    def own_arrives():
        landed(buf.at[:, z, own_rows], local_sem.at[0])
        landed(ends.at[x], local_sem.at[1])
        landed(ends.at[1 - x], x_recv.at[4])

    def limits(block, slot):
        joined = jnp.concatenate([ends[slot + portion] for portion in range(HEADS)], axis=1)
        position = lax.broadcasted_iota(jnp.int32, (1, span), 1) + block * span
        return jnp.maximum(position + 1, joined)

    key_row = lax.broadcasted_iota(jnp.int32, (span, span), 0)

    def score(kind, slot, key_block, query_block, limit=None):
        scores = dot(buf[KEY, key_block], buf[QUERY, query_block], 1, 1) * scaling
        prob_grad = dot(buf[VALUE, key_block], buf[GRAD, query_block], 1, 1)
        if limit is not None:
            scores = jnp.where(key_row + key_block * span < limit, scores, HIDDEN)
        highest = jnp.max(scores, axis=0, keepdims=True)
        probs = jnp.exp(scores - highest)
        pe[kind, slot] = probs
        pd[kind, slot] = prob_grad
        pair_stats[kind, slot, 0:1] = highest
        pair_stats[kind, slot, 1:2] = jnp.sum(probs, axis=0, keepdims=True)
        pair_stats[kind, slot, 2:3] = jnp.sum(probs * prob_grad, axis=0, keepdims=True)

    def stat(ref):
        return ref[0:1], ref[1:2], ref[2:3]

    def pair_stat(kind, slot):
        return stat(pair_stats.at[kind, slot])

    def keep(ref, value):
        for row in range(3):
            ref[row:row + 1] = value[row]

    def merge(a, b):
        highest = jnp.maximum(a[0], b[0])
        fa, fb = jnp.exp(a[0] - highest), jnp.exp(b[0] - highest)
        return highest, a[1] * fa + b[1] * fb, a[2] * fa + b[2] * fb

    def stat_copy(block, target):
        return remote(st_out.at[block], st_in.at[z, block], st_recv.at[z - 1, block - 1], target, x)

    def send_stat(block, value):
        keep(st_out.at[block], value)
        for target in range(1, blocks):
            @pl.when(takes_part(block, target) & (target != z))
            def _():
                stat_copy(block, target).start()

    def settle(block):
        keep(total, stat(st_out.at[block]))
        for source in range(1, blocks):
            @pl.when(takes_part(block, source) & (source != z))
            def _():
                landed(st_in.at[source, block], st_recv.at[source - 1, block - 1])
                keep(total, merge(stat(total), stat(st_in.at[source, block])))
        finish(block, stat(total))

    def finish(block, value):
        fin[block, 0:1] = value[0] + jnp.log(value[1])
        fin[block, 1:2] = value[2] / value[1]

    def weights(kind, slot, block):
        probs = pe[kind, slot] * jnp.exp(pair_stats[kind, slot, 0:1] - fin[block, 0:1])
        score_grad = (probs * (pd[kind, slot] - fin[block, 1:2])).astype(jnp.bfloat16)
        return probs.astype(jnp.bfloat16), score_grad

    def ret_copy(origin, slot, part, target, portion):
        return remote(
            ret_out.at[part, rows_of(portion)], ret_in.at[origin, slot, x], ret_recv.at[origin, slot],
            target, portion)

    def send_back(origin, slot, part, target, value):
        ret_out[part] = (value * scaling if slot in (DQ, DK) else value).astype(jnp.bfloat16)
        for portion in range(HEADS):
            ret_copy(origin, slot, part, target, portion).start()

    def res_copy(slot):
        return remote(res_out.at[slot], res_in.at[slot], res_recv.at[slot], z, 1 - x)

    def send_result(slot, acc):
        value = acc[other_rows, :]
        res_out[slot] = (value * scaling if slot in (DQ, DK) else value).astype(jnp.bfloat16)
        res_copy(slot).start()

    HUB, SIDE = range(2)

    def emit(slot, *origins):
        ref, acc = ((o_ref, acc_o), (dq_ref, acc_q), (dk_ref, acc_k), (dv_ref, acc_v))[slot]
        own = acc[own_rows, :]
        own = own * scaling if slot in (DQ, DK) else own
        res_copy(slot).wait_recv()
        other = res_in[slot].astype(jnp.float32)
        for origin in origins:
            landed(ret_in.at[origin, slot], ret_recv.at[origin, slot])
            own = own + ret_in[origin, slot, x].astype(jnp.float32)
            other = other + ret_in[origin, slot, 1 - x].astype(jnp.float32)
        ref[:, own_columns] = own.astype(ref.dtype)
        ref[:, other_columns] = other.astype(ref.dtype)

    def key_side(kind, slot, block, into_v, into_k):
        probs, score_grad = weights(kind, slot, block)
        into_v[...] += dot(probs, buf[GRAD, block], 1, 0)
        into_k[...] += dot(score_grad, buf[QUERY, block], 1, 0)

    @pl.when(z == 0)
    def _():
        for array in (KEY, VALUE):
            pass_on(array)
        for array in (QUERY, GRAD):
            pass_on(array)
        own_arrives()
        limit = limits(0, 0)
        score(0, 0, 0, 0, limit)
        value = pair_stat(0, 0)
        if key_back:
            key_arrives(1)
            score(1, 0, 1, 0, limit)
            value = merge(value, pair_stat(1, 0))
        finish(0, value)
        probs, score_grad = weights(0, 0, 0)
        acc_o[...] = dot(probs, buf[VALUE, 0], 0, 0)
        acc_q[...] = dot(score_grad, buf[KEY, 0], 0, 0)
        acc_v[...] = dot(probs, buf[GRAD, 0], 1, 0)
        acc_k[...] = dot(score_grad, buf[QUERY, 0], 1, 0)
        if key_back:
            probs, score_grad = weights(1, 0, 0)
            send_back(SIDE, DV, 0, 1, dot(probs, buf[GRAD, 0], 1, 0))
            send_back(SIDE, DK, 1, 1, dot(score_grad, buf[QUERY, 0], 1, 0))
            acc_o[...] += dot(probs, buf[VALUE, 1], 0, 0)
            acc_q[...] += dot(score_grad, buf[KEY, 1], 0, 0)
        send_result(DV, acc_v)
        send_result(DK, acc_k)
        send_result(OUT, acc_o)
        send_result(DQ, acc_q)
        emit(OUT)
        emit(DQ)

    @pl.when(z == 1)
    def _():
        for array in (QUERY, GRAD, KEY, VALUE):
            pass_on(array)
        own_arrives()
        score(0, 1, 1, 1, limits(1, 0))
        key_arrives(0)
        score(1, 1, 0, 1)
        send_stat(1, merge(pair_stat(0, 1), pair_stat(1, 1)))
        all_ready()

        def scores_of(block):
            query_arrives(block)
            score(1, block, 0, block)
            score(0, block, 1, block)
            send_stat(block, merge(pair_stat(0, block), pair_stat(1, block)))

        def query_side(far, far_grad, near, near_grad):
            return (
                dot(far, buf[VALUE, 0], 0, 0) + dot(near, buf[VALUE, 1], 0, 0),
                dot(far_grad, buf[KEY, 0], 0, 0) + dot(near_grad, buf[KEY, 1], 0, 0))

        alt[...] = jnp.zeros_like(alt)

        @pl.loop(2, blocks)
        def _(block):
            scores_of(block)

        @pl.loop(2, last)
        def _(block):
            settle(block)
            far, far_grad = weights(1, block, block)
            alt[0] += dot(far, buf[GRAD, block], 1, 0)
            alt[1] += dot(far_grad, buf[QUERY, block], 1, 0)
            near, near_grad = weights(0, block, block)
            output, query_grad = query_side(far, far_grad, near, near_grad)
            send_back(HUB, OUT, 2 * block, block, output)
            send_back(HUB, DQ, 2 * block + 1, block, query_grad)
        settle(1)
        key_side(1, 1, 1, alt.at[0], alt.at[1])
        settle(last)
        far, far_grad = weights(1, last, last)
        ret_out[0] = (alt[0] + dot(far, buf[GRAD, last], 1, 0)).astype(jnp.bfloat16)
        ret_copy(HUB, DV, 0, 0, 0).start()
        ret_out[1] = ((alt[1] + dot(far_grad, buf[QUERY, last], 1, 0)) * scaling).astype(jnp.bfloat16)
        ret_copy(HUB, DK, 1, 0, 0).start()
        ret_copy(HUB, DV, 0, 0, 1).start()
        ret_copy(HUB, DK, 1, 0, 1).start()
        near, near_grad = weights(0, last, last)
        output, query_grad = query_side(far, far_grad, near, near_grad)
        send_back(HUB, OUT, 2 * last, last, output)
        send_back(HUB, DQ, 2 * last + 1, last, query_grad)
        acc_v[...] = dot(near, buf[GRAD, last], 1, 0)
        acc_k[...] = dot(near_grad, buf[QUERY, last], 1, 0)

        far, far_grad = weights(1, 1, 1)
        near, near_grad = weights(0, 1, 1)
        acc_o[...], acc_q[...] = query_side(far, far_grad, near, near_grad)
        send_result(OUT, acc_o)
        send_result(DQ, acc_q)
        acc_v[...] += dot(near, buf[GRAD, 1], 1, 0)
        acc_k[...] += dot(near_grad, buf[QUERY, 1], 1, 0)

        @pl.loop(2, last)
        def _(block):
            key_side(0, block, block, acc_v, acc_k)
        send_result(DV, acc_v)
        send_result(DK, acc_k)

    @pl.when(z >= 2)
    def _():
        for array in (QUERY, GRAD, KEY, VALUE):
            pass_on(array)
        own_arrives()
        score(0, z, z, z, limits(z, 0))
        send_stat(z, pair_stat(0, z))

        @pl.when(ahead(z - 1))
        def _():
            query_arrives(z - 1)
            landed(ends.at[HEADS:2 * HEADS], end_recv)
            score(0, z - 1, z, z - 1, limits(z - 1, HEADS))
            send_stat(z - 1, pair_stat(0, z - 1))

        @pl.loop(z + 1, blocks)
        def _(block):
            query_arrives(block)
            score(0, block, z, block)
            send_stat(block, pair_stat(0, block))

        all_ready()
        acc_k[...] = jnp.zeros_like(acc_k)
        acc_v[...] = jnp.zeros_like(acc_v)
        @pl.when(ahead(z - 1))
        def _():
            settle(z - 1)
            probs, score_grad = weights(0, z - 1, z - 1)
            send_back(SIDE, OUT, 0, z - 1, dot(probs, buf[VALUE, z], 0, 0))
            send_back(SIDE, DQ, 1, z - 1, dot(score_grad, buf[KEY, z], 0, 0))
            acc_v[...] += dot(probs, buf[GRAD, z - 1], 1, 0)
            acc_k[...] += dot(score_grad, buf[QUERY, z - 1], 1, 0)

        @pl.loop(1, z - 1)
        def _(back):
            key_arrives(z - back)
            score(1, z - back, z - back, z)

        settle(z)
        probs, score_grad = weights(0, z, z)
        acc_v[...] += dot(probs, buf[GRAD, z], 1, 0)
        acc_k[...] += dot(score_grad, buf[QUERY, z], 1, 0)
        @pl.when(z == last)
        def _():
            send_result(DV, acc_v)
            send_result(DK, acc_k)
        acc_o[...] = dot(probs, buf[VALUE, z], 0, 0)
        acc_q[...] = dot(score_grad, buf[KEY, z], 0, 0)

        @pl.loop(1, z - 1)
        def _(back):
            block = z - back
            probs, score_grad = weights(1, block, z)
            acc_o[...] += dot(probs, buf[VALUE, block], 0, 0)
            acc_q[...] += dot(score_grad, buf[KEY, block], 0, 0)
        send_result(OUT, acc_o)
        send_result(DQ, acc_q)

        @pl.when(z < last)
        def _():
            @pl.loop(z + 1, blocks)
            def _(block):
                settle(block)
                key_side(0, block, block, acc_v, acc_k)
            send_result(DV, acc_v)
            send_result(DK, acc_k)

    @pl.when(z == 0)
    def _():
        all_ready()
    for _ in range(4):
        res_copy(0).wait_send()
        x_copy(0).wait_send()
    x_ends().wait_send()
    @pl.when(up_query)
    def _():
        for column in range(HEADS):
            up_ends(column).wait_send()
            for array in (QUERY, GRAD):
                query_copy(array, z + 1, column).wait_send()
    @pl.loop(1, z)
    def _(target):
        for _ in range(4):
            query_copy(QUERY, target, x).wait_send()
    @pl.when(down_key)
    def _():
        for _ in range(4):
            query_copy(KEY, 0, x).wait_send()
    @pl.loop(0, z + 1)
    def _(block):
        @pl.when(up_key(block))
        def _():
            for _ in range(4):
                array_copy(KEY, block, 0, z + 1).wait_send()
    @pl.when(z >= 1)
    def _():
        @pl.loop(jnp.maximum(z - 1, 1), blocks)
        def _(block):
            @pl.when((block >= z) | ahead(z - 1))
            def _():
                for target in range(1, blocks):
                    @pl.when(takes_part(block, target) & (target != z))
                    def _():
                        stat_copy(block, target).wait_send()
    @pl.when(((z == 0) & ahead(0)) | (z == 1) | ((z >= 2) & ahead(z - 1)))
    def _():
        for _ in range(4):
            ret_copy(HUB, OUT, 0, 0, 0).wait_send()
    @pl.when(z == 1)
    def _():
        @pl.loop(2, blocks)
        def _(block):
            for _ in range(4):
                ret_copy(HUB, OUT, 0, 0, 0).wait_send()

    @pl.when(z == 0)
    def _():
        emit(DV, HUB)
        emit(DK, HUB)
    @pl.when(z == 1)
    def _():
        for slot in (OUT, DQ):
            emit(slot, *((SIDE,) if query_back else ()))
        for slot in (DV, DK):
            emit(slot, *((SIDE,) if key_back else ()))
    @pl.when(z >= 2)
    def _():
        @pl.when(ahead(z))
        def _():
            emit(OUT, HUB, SIDE)
            emit(DQ, HUB, SIDE)
        @pl.when(jnp.logical_not(ahead(z)))
        def _():
            emit(OUT, HUB)
            emit(DQ, HUB)
        emit(DV)
        emit(DK)


def flush(*refs):
    sem = refs[-1]
    copies = [pltpu.make_async_copy(refs[i], refs[i + 4], sem.at[i]) for i in range(4)]
    for copy in copies:
        copy.start()
    for copy in copies:
        copy.wait()


def solution(mesh):
    n = mesh.shape["ctx"]

    def local(queries, keys, values, out_grad, span_end):
        rows = queries.shape[0]
        blocks, span = n // HEADS, HEADS * rows
        f32, bf16 = jnp.float32, jnp.bfloat16
        anywhere = pl.BlockSpec(memory_space=pl.ANY)
        vmem = pl.BlockSpec(memory_space=pltpu.VMEM)
        dma = pltpu.SemaphoreType.DMA
        results = pl.pallas_call(
            functools.partial(kernel, n, rows),
            out_shape=tuple(
                pltpu.VMEM(queries.shape, kind) for kind in (bf16, f32, f32, f32)),
            in_specs=[anywhere] * 5,
            out_specs=(vmem,) * 4,
            scratch_shapes=[
                pltpu.VMEM((4, blocks, span, HEAD_DIM), bf16),
                pltpu.VMEM((2 * HEADS, 1, rows), jnp.int32),
                pltpu.VMEM((2, blocks, span, span), f32),
                pltpu.VMEM((2, blocks, span, span), f32),
                pltpu.VMEM((2, blocks, 3, span), f32),
                pltpu.VMEM((blocks, blocks, 3, span), f32),
                pltpu.VMEM((blocks, 3, span), f32),
                pltpu.VMEM((3, span), f32),
                pltpu.VMEM((blocks, 2, span), f32),
                pltpu.VMEM((span, HEAD_DIM), f32),
                pltpu.VMEM((span, HEAD_DIM), f32),
                pltpu.VMEM((span, HEAD_DIM), f32),
                pltpu.VMEM((span, HEAD_DIM), f32),
                pltpu.VMEM((2, span, HEAD_DIM), f32),
                pltpu.VMEM((2 * blocks, span, HEAD_DIM), bf16),
                pltpu.VMEM((2, 4, HEADS, rows, HEAD_DIM), bf16),
                pltpu.VMEM((4, rows, HEAD_DIM), bf16),
                pltpu.VMEM((4, rows, HEAD_DIM), bf16),
                dma((2,)),
                dma((5,)),
                dma((2, blocks)),
                dma,
                dma((blocks - 1, blocks - 1)),
                dma((2, 4)),
                dma((4,)),
                dma,
                pltpu.SemaphoreType.REGULAR((blocks - 1,)),
            ],
            compiler_params=pltpu.CompilerParams(collective_id=0, has_side_effects=True),
        )(queries, keys, values, out_grad, span_end[None])
        return pl.pallas_call(
            flush,
            out_shape=tuple(
                jax.ShapeDtypeStruct(queries.shape, kind) for kind in (bf16, f32, f32, f32)),
            in_specs=[vmem] * 4,
            out_specs=(anywhere,) * 4,
            scratch_shapes=[dma((4,))],
        )(*(pltpu.with_memory_space_constraint(result, pltpu.VMEM) for result in results))

    spec = P(("dp", "ctx"), None)
    return jax.shard_map(
        local, mesh=mesh, in_specs=(spec,) * 4 + (P(("dp", "ctx")),),
        out_specs=(spec,) * 4, check_vma=False)
```

```python
import functools

import jax
import jax.numpy as jnp
from jax import lax
from jax.experimental import pallas as pl
from jax.experimental.pallas import tpu as pltpu
from jax.sharding import PartitionSpec as P

HEADS = 2
HEAD_DIM = 128
IMG = 288
HIDDEN = -1e30
KEY, VALUE, QUERY, GRAD = range(4)


def dot(a, b, a_dim, b_dim):
    return lax.dot_general(a, b, (((a_dim,), (b_dim,)), ((), ())), preferred_element_type=jnp.float32)


def kernel(
    n, rows,
    q_in, k_in, v_in, g_in, ends_in,
    o_ref, dq_ref, dk_ref, dv_ref,
    buf, ends, pe, pd, pair_stats, st_in, st_out, total, fin,
    acc_o, acc_q, acc_k, acc_v, alt, ret_out, ret_in, res_out, res_in,
    local_sem, x_recv, z_recv, end_recv, st_recv, ret_recv, res_recv, sent, ready,
):
    scaling = HEAD_DIM ** -0.5
    blocks = n // HEADS
    span = HEADS * rows
    cut = blocks * span - IMG
    last = blocks - 1
    me = lax.axis_index("ctx")
    z = me // HEADS
    x = me % HEADS
    sources = (k_in, v_in, q_in, g_in)
    OUT, DQ, DK, DV = range(4)

    def device(block, column):
        return {"ctx": block * HEADS + column}

    def ahead(block):
        return ((block + 1) * span < cut) & (block + 1 < blocks)

    def rows_of(portion):
        return pl.ds(pl.multiple_of(portion * rows, 16), rows)

    def columns_of(head):
        return pl.ds(pl.multiple_of(head * HEAD_DIM, HEAD_DIM), HEAD_DIM)

    own_rows, other_rows = rows_of(x), rows_of(1 - x)
    own_columns, other_columns = columns_of(x), columns_of(1 - x)

    key_back = span < cut
    query_back = 2 * span < cut and last > 1
    down_key = (z == 1) & ahead(0)
    up_query = (z >= 1) & ahead(z)

    def up_key(block):
        return (z < last) & ((z == 0) | (block >= 2))

    def takes_part(block, target):
        return (target >= 1) & ((target <= block) | ((target == block + 1) & ahead(block)))

    barrier = pltpu.get_barrier_semaphore()
    for target in range(1, blocks):
        @pl.when(target > z)
        def _():
            for column in range(HEADS):
                pl.semaphore_signal(barrier, inc=1, device_id=device(target, column))
    pl.semaphore_signal(barrier, inc=1, device_id=device(z, 1 - x))

    def own_copy(array):
        return pltpu.make_async_copy(
            sources[array].at[:, own_columns], buf.at[array, z, own_rows], local_sem.at[0])

    for array in range(4):
        own_copy(array).start()
    pltpu.make_async_copy(ends_in, ends.at[x], local_sem.at[1]).start()

    pl.semaphore_wait(barrier, HEADS * z + 1)
    for target in range(last):
        @pl.when(target < z)
        def _():
            for column in range(HEADS):
                pl.semaphore_signal(ready.at[z - 1], inc=1, device_id=device(target, column))

    def remote(src, dst, recv, target, column):
        return pltpu.make_async_remote_copy(
            src_ref=src, dst_ref=dst, send_sem=sent, recv_sem=recv, device_id=device(target, column))

    def array_copy(array, block, portion, target, own=False):
        dst = buf.at[array, block, rows_of(portion)]
        return remote(
            sources[array].at[:, own_columns] if own else dst, dst,
            z_recv.at[array // 2, block], target, x)

    def query_copy(array, target, column):
        return remote(
            sources[array].at[:, columns_of(column)], buf.at[array, z, own_rows],
            z_recv.at[array // 2, z], target, column)

    def x_copy(array):
        return remote(
            sources[array].at[:, other_columns], buf.at[array, z, own_rows], x_recv.at[array], z, 1 - x)

    def x_ends():
        return remote(ends_in, ends.at[x], x_recv.at[4], z, 1 - x)

    def up_ends(column):
        return remote(ends_in, ends.at[HEADS + x], end_recv, z + 1, column)

    def landed(ref, sem):
        pltpu.make_async_copy(ref, ref, sem).wait()

    def send_query(target):
        for column in (x, 1 - x):
            for array in (QUERY, GRAD):
                query_copy(array, target, column).start()

    def send_key(array, portion, own):
        @pl.when(up_key(z))
        def _():
            array_copy(array, z, portion, z + 1, own).start()

    @pl.when(z == 0)
    def _():
        for array in (KEY, VALUE, QUERY, GRAD):
            x_copy(array).start()
    @pl.when(z > 0)
    def _():
        for array in (QUERY, GRAD, KEY, VALUE):
            x_copy(array).start()
    for target in range(last - 1, 0, -1):
        @pl.when((target < z) & (z > 2))
        def _():
            for array in (QUERY, GRAD):
                query_copy(array, target, x).start()
    @pl.when(z == 2)
    def _():
        send_query(1)
    @pl.when(down_key)
    def _():
        for column in (x, 1 - x):
            for array in (KEY, VALUE):
                query_copy(array, 0, column).start()
    x_ends().start()

    @pl.when(z < last)
    def _():
        pl.semaphore_wait(ready.at[z], HEADS)
    for target in range(2, blocks):
        @pl.when(up_query & (target == z + 1))
        def _():
            for column in range(HEADS):
                up_ends(column).start()
            for array in (QUERY, GRAD):
                query_copy(array, target, x).start()
    @pl.when(z == 0)
    def _():
        for array in (KEY, VALUE):
            send_key(array, x, True)

    def all_ready():
        @pl.loop(z + 2, blocks)
        def _(target):
            pl.semaphore_wait(ready.at[target - 1], HEADS)

    def pass_on(array):
        landed(buf.at[array, z, other_rows], x_recv.at[array])
        if array in (KEY, VALUE):
            @pl.when(z > 0)
            def _():
                send_key(array, x, True)
            send_key(array, 1 - x, False)
        else:
            @pl.when(up_query)
            def _():
                array_copy(array, z, 1 - x, z + 1).start()
            @pl.when(z > 2)
            def _():
                array_copy(array, z, 1 - x, z - 1).start()
                if array == GRAD:
                    for target in range(last - 2, 0, -1):
                        @pl.when(target < z - 1)
                        def _():
                            for half in (QUERY, GRAD):
                                array_copy(half, z, 1 - x, target).start()

    def key_arrives(block):
        landed(buf.at[KEY:VALUE + 1, block], z_recv.at[0, block])
        @pl.when(up_key(block) & (block < z))
        def _():
            for array in (KEY, VALUE):
                for portion in range(HEADS):
                    array_copy(array, block, portion, z + 1).start()

    def query_arrives(block):
        landed(buf.at[QUERY:GRAD + 1, block], z_recv.at[1, block])

    def own_arrives():
        landed(buf.at[:, z, own_rows], local_sem.at[0])
        landed(ends.at[x], local_sem.at[1])
        landed(ends.at[1 - x], x_recv.at[4])

    def limits(block, slot):
        joined = jnp.concatenate([ends[slot + portion] for portion in range(HEADS)], axis=1)
        position = lax.broadcasted_iota(jnp.int32, (1, span), 1) + block * span
        return jnp.maximum(position + 1, joined)

    key_row = lax.broadcasted_iota(jnp.int32, (span, span), 0)

    def score(kind, slot, key_block, query_block, limit=None):
        scores = dot(buf[KEY, key_block], buf[QUERY, query_block], 1, 1) * scaling
        prob_grad = dot(buf[VALUE, key_block], buf[GRAD, query_block], 1, 1)
        if limit is not None:
            scores = jnp.where(key_row + key_block * span < limit, scores, HIDDEN)
        highest = jnp.max(scores, axis=0, keepdims=True)
        probs = jnp.exp(scores - highest)
        pe[kind, slot] = probs
        pd[kind, slot] = prob_grad
        pair_stats[kind, slot, 0:1] = highest
        pair_stats[kind, slot, 1:2] = jnp.sum(probs, axis=0, keepdims=True)
        pair_stats[kind, slot, 2:3] = jnp.sum(probs * prob_grad, axis=0, keepdims=True)

    def stat(ref):
        return ref[0:1], ref[1:2], ref[2:3]

    def pair_stat(kind, slot):
        return stat(pair_stats.at[kind, slot])

    def keep(ref, value):
        for row in range(3):
            ref[row:row + 1] = value[row]

    def merge(a, b):
        highest = jnp.maximum(a[0], b[0])
        fa, fb = jnp.exp(a[0] - highest), jnp.exp(b[0] - highest)
        return highest, a[1] * fa + b[1] * fb, a[2] * fa + b[2] * fb

    def stat_copy(block, target):
        return remote(st_out.at[block], st_in.at[z, block], st_recv.at[z - 1, block - 1], target, x)

    def send_stat(block, value):
        keep(st_out.at[block], value)
        for target in range(1, blocks):
            @pl.when(takes_part(block, target) & (target != z))
            def _():
                stat_copy(block, target).start()

    def settle(block):
        keep(total, stat(st_out.at[block]))
        for source in range(1, blocks):
            @pl.when(takes_part(block, source) & (source != z))
            def _():
                landed(st_in.at[source, block], st_recv.at[source - 1, block - 1])
                keep(total, merge(stat(total), stat(st_in.at[source, block])))
        finish(block, stat(total))

    def finish(block, value):
        fin[block, 0:1] = value[0] + jnp.log(value[1])
        fin[block, 1:2] = value[2] / value[1]

    def weights(kind, slot, block):
        probs = pe[kind, slot] * jnp.exp(pair_stats[kind, slot, 0:1] - fin[block, 0:1])
        score_grad = (probs * (pd[kind, slot] - fin[block, 1:2])).astype(jnp.bfloat16)
        return probs.astype(jnp.bfloat16), score_grad

    def ret_copy(origin, slot, part, target, portion):
        return remote(
            ret_out.at[part, rows_of(portion)], ret_in.at[origin, slot, x], ret_recv.at[origin, slot],
            target, portion)

    def hold_back(slot, part, value):
        ret_out[part] = (value * scaling if slot in (DQ, DK) else value).astype(jnp.bfloat16)

    def send_back(origin, slot, part, target, value):
        hold_back(slot, part, value)
        for portion in range(HEADS):
            ret_copy(origin, slot, part, target, portion).start()

    def res_copy(slot):
        return remote(res_out.at[slot], res_in.at[slot], res_recv.at[slot], z, 1 - x)

    def send_result(slot, acc):
        value = acc[other_rows, :]
        res_out[slot] = (value * scaling if slot in (DQ, DK) else value).astype(jnp.bfloat16)
        res_copy(slot).start()

    HUB, SIDE = range(2)

    def emit(slot, *origins):
        ref, acc = ((o_ref, acc_o), (dq_ref, acc_q), (dk_ref, acc_k), (dv_ref, acc_v))[slot]
        own = acc[own_rows, :]
        own = own * scaling if slot in (DQ, DK) else own
        res_copy(slot).wait_recv()
        other = res_in[slot].astype(jnp.float32)
        for origin in origins:
            landed(ret_in.at[origin, slot], ret_recv.at[origin, slot])
            own = own + ret_in[origin, slot, x].astype(jnp.float32)
            other = other + ret_in[origin, slot, 1 - x].astype(jnp.float32)
        ref[:, own_columns] = own.astype(ref.dtype)
        ref[:, other_columns] = other.astype(ref.dtype)

    def key_side(kind, slot, block, into_v, into_k):
        probs, score_grad = weights(kind, slot, block)
        into_v[...] += dot(probs, buf[GRAD, block], 1, 0)
        into_k[...] += dot(score_grad, buf[QUERY, block], 1, 0)

    @pl.when(z == 0)
    def _():
        for array in (KEY, VALUE):
            pass_on(array)
        for array in (QUERY, GRAD):
            pass_on(array)
        own_arrives()
        limit = limits(0, 0)
        score(0, 0, 0, 0, limit)
        value = pair_stat(0, 0)
        if key_back:
            key_arrives(1)
            score(1, 0, 1, 0, limit)
            value = merge(value, pair_stat(1, 0))
        finish(0, value)
        probs, score_grad = weights(0, 0, 0)
        acc_o[...] = dot(probs, buf[VALUE, 0], 0, 0)
        acc_q[...] = dot(score_grad, buf[KEY, 0], 0, 0)
        acc_v[...] = dot(probs, buf[GRAD, 0], 1, 0)
        acc_k[...] = dot(score_grad, buf[QUERY, 0], 1, 0)
        if key_back:
            probs, score_grad = weights(1, 0, 0)
            send_back(SIDE, DV, 0, 1, dot(probs, buf[GRAD, 0], 1, 0))
            send_back(SIDE, DK, 1, 1, dot(score_grad, buf[QUERY, 0], 1, 0))
            acc_o[...] += dot(probs, buf[VALUE, 1], 0, 0)
            acc_q[...] += dot(score_grad, buf[KEY, 1], 0, 0)
        send_result(DV, acc_v)
        send_result(DK, acc_k)
        send_result(OUT, acc_o)
        send_result(DQ, acc_q)
        emit(OUT)
        emit(DQ)

    @pl.when(z == 1)
    def _():
        for array in (QUERY, GRAD, KEY, VALUE):
            pass_on(array)
        own_arrives()
        score(0, 1, 1, 1, limits(1, 0))
        key_arrives(0)
        score(1, 1, 0, 1)
        send_stat(1, merge(pair_stat(0, 1), pair_stat(1, 1)))
        all_ready()

        def scores_of(block):
            query_arrives(block)
            score(1, block, 0, block)
            score(0, block, 1, block)
            send_stat(block, merge(pair_stat(0, block), pair_stat(1, block)))

        def query_side(far, far_grad, near, near_grad):
            return (
                dot(far, buf[VALUE, 0], 0, 0) + dot(near, buf[VALUE, 1], 0, 0),
                dot(far_grad, buf[KEY, 0], 0, 0) + dot(near_grad, buf[KEY, 1], 0, 0))

        alt[...] = jnp.zeros_like(alt)

        alt[...] = jnp.zeros_like(alt)

        def finish_block(block):
            settle(block)
            far, far_grad = weights(1, block, block)
            alt[0] += dot(far, buf[GRAD, block], 1, 0)
            alt[1] += dot(far_grad, buf[QUERY, block], 1, 0)
            near, near_grad = weights(0, block, block)
            output, query_grad = query_side(far, far_grad, near, near_grad)
            hold_back(OUT, 2 * block, output)
            hold_back(DQ, 2 * block + 1, query_grad)

        pl.loop(2, last)(scores_of)
        pl.loop(2, last)(finish_block)
        scores_of(last)
        @pl.loop(2, last)
        def _(block):
            for part, slot in enumerate((OUT, DQ)):
                for portion in range(HEADS):
                    ret_copy(HUB, slot, 2 * block + part, block, portion).start()
        settle(1)
        key_side(1, 1, 1, alt.at[0], alt.at[1])
        settle(last)
        far, far_grad = weights(1, last, last)
        ret_out[0] = (alt[0] + dot(far, buf[GRAD, last], 1, 0)).astype(jnp.bfloat16)
        ret_copy(HUB, DV, 0, 0, 0).start()
        ret_out[1] = ((alt[1] + dot(far_grad, buf[QUERY, last], 1, 0)) * scaling).astype(jnp.bfloat16)
        ret_copy(HUB, DK, 1, 0, 0).start()
        ret_copy(HUB, DV, 0, 0, 1).start()
        ret_copy(HUB, DK, 1, 0, 1).start()
        near, near_grad = weights(0, last, last)
        output, query_grad = query_side(far, far_grad, near, near_grad)
        send_back(HUB, OUT, 2 * last, last, output)
        send_back(HUB, DQ, 2 * last + 1, last, query_grad)
        acc_v[...] = dot(near, buf[GRAD, last], 1, 0)
        acc_k[...] = dot(near_grad, buf[QUERY, last], 1, 0)

        far, far_grad = weights(1, 1, 1)
        near, near_grad = weights(0, 1, 1)
        acc_o[...], acc_q[...] = query_side(far, far_grad, near, near_grad)
        send_result(OUT, acc_o)
        send_result(DQ, acc_q)
        acc_v[...] += dot(near, buf[GRAD, 1], 1, 0)
        acc_k[...] += dot(near_grad, buf[QUERY, 1], 1, 0)

        @pl.loop(2, last)
        def _(block):
            key_side(0, block, block, acc_v, acc_k)
        send_result(DV, acc_v)
        send_result(DK, acc_k)

    @pl.when(z >= 2)
    def _():
        for array in (QUERY, GRAD, KEY, VALUE):
            pass_on(array)
        own_arrives()
        score(0, z, z, z, limits(z, 0))
        send_stat(z, pair_stat(0, z))

        @pl.when(ahead(z - 1))
        def _():
            query_arrives(z - 1)
            landed(ends.at[HEADS:2 * HEADS], end_recv)
            score(0, z - 1, z, z - 1, limits(z - 1, HEADS))
            send_stat(z - 1, pair_stat(0, z - 1))

        @pl.loop(z + 1, blocks)
        def _(block):
            query_arrives(block)
            score(0, block, z, block)
            send_stat(block, pair_stat(0, block))

        all_ready()
        acc_k[...] = jnp.zeros_like(acc_k)
        acc_v[...] = jnp.zeros_like(acc_v)
        @pl.when(ahead(z - 1))
        def _():
            settle(z - 1)
            probs, score_grad = weights(0, z - 1, z - 1)
            send_back(SIDE, OUT, 0, z - 1, dot(probs, buf[VALUE, z], 0, 0))
            send_back(SIDE, DQ, 1, z - 1, dot(score_grad, buf[KEY, z], 0, 0))
            acc_v[...] += dot(probs, buf[GRAD, z - 1], 1, 0)
            acc_k[...] += dot(score_grad, buf[QUERY, z - 1], 1, 0)

        @pl.loop(1, z - 1)
        def _(back):
            key_arrives(z - back)
            score(1, z - back, z - back, z)

        settle(z)
        probs, score_grad = weights(0, z, z)
        acc_v[...] += dot(probs, buf[GRAD, z], 1, 0)
        acc_k[...] += dot(score_grad, buf[QUERY, z], 1, 0)
        @pl.when(z == last)
        def _():
            send_result(DV, acc_v)
            send_result(DK, acc_k)
        acc_o[...] = dot(probs, buf[VALUE, z], 0, 0)
        acc_q[...] = dot(score_grad, buf[KEY, z], 0, 0)

        @pl.loop(1, z - 1)
        def _(back):
            block = z - back
            probs, score_grad = weights(1, block, z)
            acc_o[...] += dot(probs, buf[VALUE, block], 0, 0)
            acc_q[...] += dot(score_grad, buf[KEY, block], 0, 0)
        send_result(OUT, acc_o)
        send_result(DQ, acc_q)

        @pl.when(z < last)
        def _():
            @pl.loop(z + 1, blocks)
            def _(block):
                settle(block)
                key_side(0, block, block, acc_v, acc_k)
            send_result(DV, acc_v)
            send_result(DK, acc_k)

    @pl.when(z == 0)
    def _():
        all_ready()
    for _ in range(4):
        res_copy(0).wait_send()
        x_copy(0).wait_send()
    x_ends().wait_send()
    @pl.when(up_query)
    def _():
        for column in range(HEADS):
            up_ends(column).wait_send()
            for array in (QUERY, GRAD):
                query_copy(array, z + 1, column).wait_send()
    @pl.loop(1, z)
    def _(target):
        for _ in range(4):
            query_copy(QUERY, target, x).wait_send()
    @pl.when(down_key)
    def _():
        for _ in range(4):
            query_copy(KEY, 0, x).wait_send()
    @pl.loop(0, z + 1)
    def _(block):
        @pl.when(up_key(block))
        def _():
            for _ in range(4):
                array_copy(KEY, block, 0, z + 1).wait_send()
    @pl.when(z >= 1)
    def _():
        @pl.loop(jnp.maximum(z - 1, 1), blocks)
        def _(block):
            @pl.when((block >= z) | ahead(z - 1))
            def _():
                for target in range(1, blocks):
                    @pl.when(takes_part(block, target) & (target != z))
                    def _():
                        stat_copy(block, target).wait_send()
    @pl.when(((z == 0) & ahead(0)) | (z == 1) | ((z >= 2) & ahead(z - 1)))
    def _():
        for _ in range(4):
            ret_copy(HUB, OUT, 0, 0, 0).wait_send()
    @pl.when(z == 1)
    def _():
        @pl.loop(2, blocks)
        def _(block):
            for _ in range(4):
                ret_copy(HUB, OUT, 0, 0, 0).wait_send()

    @pl.when(z == 0)
    def _():
        emit(DV, HUB)
        emit(DK, HUB)
    @pl.when(z == 1)
    def _():
        for slot in (OUT, DQ):
            emit(slot, *((SIDE,) if query_back else ()))
        for slot in (DV, DK):
            emit(slot, *((SIDE,) if key_back else ()))
    @pl.when(z >= 2)
    def _():
        @pl.when(ahead(z))
        def _():
            emit(OUT, HUB, SIDE)
            emit(DQ, HUB, SIDE)
        @pl.when(jnp.logical_not(ahead(z)))
        def _():
            emit(OUT, HUB)
            emit(DQ, HUB)
        emit(DV)
        emit(DK)


def flush(*refs):
    sem = refs[-1]
    copies = [pltpu.make_async_copy(refs[i], refs[i + 4], sem.at[i]) for i in range(4)]
    for copy in copies:
        copy.start()
    for copy in copies:
        copy.wait()


def solution(mesh):
    n = mesh.shape["ctx"]

    def local(queries, keys, values, out_grad, span_end):
        rows = queries.shape[0]
        blocks, span = n // HEADS, HEADS * rows
        f32, bf16 = jnp.float32, jnp.bfloat16
        anywhere = pl.BlockSpec(memory_space=pl.ANY)
        vmem = pl.BlockSpec(memory_space=pltpu.VMEM)
        dma = pltpu.SemaphoreType.DMA
        results = pl.pallas_call(
            functools.partial(kernel, n, rows),
            out_shape=tuple(
                pltpu.VMEM(queries.shape, kind) for kind in (bf16, f32, f32, f32)),
            in_specs=[anywhere] * 5,
            out_specs=(vmem,) * 4,
            scratch_shapes=[
                pltpu.VMEM((4, blocks, span, HEAD_DIM), bf16),
                pltpu.VMEM((2 * HEADS, 1, rows), jnp.int32),
                pltpu.VMEM((2, blocks, span, span), f32),
                pltpu.VMEM((2, blocks, span, span), f32),
                pltpu.VMEM((2, blocks, 3, span), f32),
                pltpu.VMEM((blocks, blocks, 3, span), f32),
                pltpu.VMEM((blocks, 3, span), f32),
                pltpu.VMEM((3, span), f32),
                pltpu.VMEM((blocks, 2, span), f32),
                pltpu.VMEM((span, HEAD_DIM), f32),
                pltpu.VMEM((span, HEAD_DIM), f32),
                pltpu.VMEM((span, HEAD_DIM), f32),
                pltpu.VMEM((span, HEAD_DIM), f32),
                pltpu.VMEM((2, span, HEAD_DIM), f32),
                pltpu.VMEM((2 * blocks, span, HEAD_DIM), bf16),
                pltpu.VMEM((2, 4, HEADS, rows, HEAD_DIM), bf16),
                pltpu.VMEM((4, rows, HEAD_DIM), bf16),
                pltpu.VMEM((4, rows, HEAD_DIM), bf16),
                dma((2,)),
                dma((5,)),
                dma((2, blocks)),
                dma,
                dma((blocks - 1, blocks - 1)),
                dma((2, 4)),
                dma((4,)),
                dma,
                pltpu.SemaphoreType.REGULAR((blocks - 1,)),
            ],
            compiler_params=pltpu.CompilerParams(collective_id=0, has_side_effects=True),
        )(queries, keys, values, out_grad, span_end[None])
        return pl.pallas_call(
            flush,
            out_shape=tuple(
                jax.ShapeDtypeStruct(queries.shape, kind) for kind in (bf16, f32, f32, f32)),
            in_specs=[vmem] * 4,
            out_specs=(anywhere,) * 4,
            scratch_shapes=[dma((4,))],
        )(*(pltpu.with_memory_space_constraint(result, pltpu.VMEM) for result in results))

    spec = P(("dp", "ctx"), None)
    return jax.shard_map(
        local, mesh=mesh, in_specs=(spec,) * 4 + (P(("dp", "ctx")),),
        out_specs=(spec,) * 4, check_vma=False)
```

```python
import functools
import math

import jax
import jax.numpy as jnp
from jax import lax
from jax.experimental import pallas as pl
from jax.experimental.pallas import tpu as pltpu
from jax.sharding import PartitionSpec as P

HEADS = 2
HEAD_DIM = 128
IMG = 288
HIDDEN = -1e30
KEY, VALUE, QUERY, GRAD = range(4)


def dot(a, b, a_dim, b_dim):
    return lax.dot_general(a, b, (((a_dim,), (b_dim,)), ((), ())), preferred_element_type=jnp.float32)


def kernel(
    n, rows,
    q_in, k_in, v_in, g_in, ends_in,
    o_ref, dq_ref, dk_ref, dv_ref,
    buf, ends, pe, pd, pair_stats, st_in, st_out, total, fin,
    acc_o, acc_q, acc_k, acc_v, alt, ret_out, ret_in, res_out, res_in,
    local_sem, x_recv, z_recv, end_recv, st_recv, ret_recv, res_recv, sent, ready,
):
    scaling = HEAD_DIM ** -0.5
    binary = scaling / math.log(2.0)
    blocks = n // HEADS
    span = HEADS * rows
    cut = blocks * span - IMG
    last = blocks - 1
    me = lax.axis_index("ctx")
    z = me // HEADS
    x = me % HEADS
    sources = (k_in, v_in, q_in, g_in)
    OUT, DQ, DK, DV = range(4)

    def device(block, column):
        return {"ctx": block * HEADS + column}

    def ahead(block):
        return ((block + 1) * span < cut) & (block + 1 < blocks)

    def rows_of(portion):
        return pl.ds(pl.multiple_of(portion * rows, 16), rows)

    def columns_of(head):
        return pl.ds(pl.multiple_of(head * HEAD_DIM, HEAD_DIM), HEAD_DIM)

    own_rows, other_rows = rows_of(x), rows_of(1 - x)
    own_columns, other_columns = columns_of(x), columns_of(1 - x)

    key_back = span < cut
    query_back = 2 * span < cut and last > 1
    down_key = (z == 1) & ahead(0)
    up_query = (z >= 1) & ahead(z)

    def up_key(block):
        return (z < last) & ((z == 0) | (block >= 2))

    def takes_part(block, target):
        return (target >= 1) & ((target <= block) | ((target == block + 1) & ahead(block)))

    barrier = pltpu.get_barrier_semaphore()
    for target in range(1, blocks):
        @pl.when(target > z)
        def _():
            for column in range(HEADS):
                pl.semaphore_signal(barrier, inc=1, device_id=device(target, column))
    pl.semaphore_signal(barrier, inc=1, device_id=device(z, 1 - x))

    def own_copy(array):
        return pltpu.make_async_copy(
            sources[array].at[:, own_columns], buf.at[array, z, own_rows], local_sem.at[0])

    for array in range(4):
        own_copy(array).start()
    pltpu.make_async_copy(ends_in, ends.at[x], local_sem.at[1]).start()

    pl.semaphore_wait(barrier, HEADS * z + 1)
    for target in range(last):
        @pl.when(target < z)
        def _():
            for column in range(HEADS):
                pl.semaphore_signal(ready.at[z - 1], inc=1, device_id=device(target, column))

    def remote(src, dst, recv, target, column):
        return pltpu.make_async_remote_copy(
            src_ref=src, dst_ref=dst, send_sem=sent, recv_sem=recv, device_id=device(target, column))

    def array_copy(array, block, portion, target, own=False):
        dst = buf.at[array, block, rows_of(portion)]
        return remote(
            sources[array].at[:, own_columns] if own else dst, dst,
            z_recv.at[array // 2, block], target, x)

    def query_copy(array, target, column):
        return remote(
            sources[array].at[:, columns_of(column)], buf.at[array, z, own_rows],
            z_recv.at[array // 2, z], target, column)

    def x_copy(array):
        return remote(
            sources[array].at[:, other_columns], buf.at[array, z, own_rows], x_recv.at[array], z, 1 - x)

    def x_ends():
        return remote(ends_in, ends.at[x], x_recv.at[4], z, 1 - x)

    def up_ends(column):
        return remote(ends_in, ends.at[HEADS + x], end_recv, z + 1, column)

    def landed(ref, sem):
        pltpu.make_async_copy(ref, ref, sem).wait()

    def send_query(target):
        for column in (x, 1 - x):
            for array in (QUERY, GRAD):
                query_copy(array, target, column).start()

    def send_key(array, portion, own):
        @pl.when(up_key(z))
        def _():
            array_copy(array, z, portion, z + 1, own).start()

    @pl.when(z == 0)
    def _():
        for array in (KEY, VALUE, QUERY, GRAD):
            x_copy(array).start()
    @pl.when(z > 0)
    def _():
        for array in (QUERY, GRAD, KEY, VALUE):
            x_copy(array).start()
    for target in range(last - 1, 0, -1):
        @pl.when((target < z) & (z > 2))
        def _():
            for array in (QUERY, GRAD):
                query_copy(array, target, x).start()
    @pl.when(z == 2)
    def _():
        send_query(1)
    @pl.when(down_key)
    def _():
        for column in (x, 1 - x):
            for array in (KEY, VALUE):
                query_copy(array, 0, column).start()
    x_ends().start()

    @pl.when(z < last)
    def _():
        pl.semaphore_wait(ready.at[z], HEADS)
    for target in range(2, blocks):
        @pl.when(up_query & (target == z + 1))
        def _():
            for column in range(HEADS):
                up_ends(column).start()
            for array in (QUERY, GRAD):
                query_copy(array, target, x).start()
    @pl.when(z == 0)
    def _():
        for array in (KEY, VALUE):
            send_key(array, x, True)

    def all_ready():
        @pl.loop(z + 2, blocks)
        def _(target):
            pl.semaphore_wait(ready.at[target - 1], HEADS)

    def pass_on(array):
        landed(buf.at[array, z, other_rows], x_recv.at[array])
        if array in (KEY, VALUE):
            @pl.when(z > 0)
            def _():
                send_key(array, x, True)
            send_key(array, 1 - x, False)
        else:
            @pl.when(up_query)
            def _():
                array_copy(array, z, 1 - x, z + 1).start()
            @pl.when(z > 2)
            def _():
                array_copy(array, z, 1 - x, z - 1).start()
                if array == GRAD:
                    for target in range(last - 2, 0, -1):
                        @pl.when(target < z - 1)
                        def _():
                            for half in (QUERY, GRAD):
                                array_copy(half, z, 1 - x, target).start()

    def key_arrives(block):
        landed(buf.at[KEY:VALUE + 1, block], z_recv.at[0, block])
        @pl.when(up_key(block) & (block < z))
        def _():
            for array in (KEY, VALUE):
                for portion in range(HEADS):
                    array_copy(array, block, portion, z + 1).start()

    def query_arrives(block):
        landed(buf.at[QUERY:GRAD + 1, block], z_recv.at[1, block])

    def own_arrives():
        landed(buf.at[:, z, own_rows], local_sem.at[0])
        landed(ends.at[x], local_sem.at[1])
        landed(ends.at[1 - x], x_recv.at[4])

    def limits(block, slot):
        joined = jnp.concatenate([ends[slot + portion] for portion in range(HEADS)], axis=1)
        position = lax.broadcasted_iota(jnp.int32, (1, span), 1) + block * span
        return jnp.maximum(position + 1, joined)

    key_row = lax.broadcasted_iota(jnp.int32, (span, span), 0)

    def score(kind, slot, key_block, query_block, limit=None):
        scores = dot(buf[KEY, key_block], buf[QUERY, query_block], 1, 1)
        prob_grad = dot(buf[VALUE, key_block], buf[GRAD, query_block], 1, 1)
        if limit is not None:
            scores = jnp.where(key_row + key_block * span < limit, scores, HIDDEN)
        highest = jnp.max(scores, axis=0, keepdims=True)
        probs = jnp.exp2((scores - highest) * binary)
        pe[kind, slot] = probs
        pd[kind, slot] = prob_grad
        pair_stats[kind, slot, 0:1] = highest * binary
        pair_stats[kind, slot, 1:2] = jnp.sum(probs, axis=0, keepdims=True)
        pair_stats[kind, slot, 2:3] = jnp.sum(probs * prob_grad, axis=0, keepdims=True)

    def stat(ref):
        return ref[0:1], ref[1:2], ref[2:3]

    def pair_stat(kind, slot):
        return stat(pair_stats.at[kind, slot])

    def keep(ref, value):
        for row in range(3):
            ref[row:row + 1] = value[row]

    def merge(a, b):
        highest = jnp.maximum(a[0], b[0])
        fa, fb = jnp.exp2(a[0] - highest), jnp.exp2(b[0] - highest)
        return highest, a[1] * fa + b[1] * fb, a[2] * fa + b[2] * fb

    def stat_copy(block, target):
        return remote(st_out.at[block], st_in.at[z, block], st_recv.at[z - 1, block - 1], target, x)

    def send_stat(block, value):
        keep(st_out.at[block], value)
        for target in range(1, blocks):
            @pl.when(takes_part(block, target) & (target != z))
            def _():
                stat_copy(block, target).start()

    def settle(block):
        keep(total, stat(st_out.at[block]))
        for source in range(1, blocks):
            @pl.when(takes_part(block, source) & (source != z))
            def _():
                landed(st_in.at[source, block], st_recv.at[source - 1, block - 1])
                keep(total, merge(stat(total), stat(st_in.at[source, block])))
        finish(block, stat(total))

    def finish(block, value):
        fin[block, 0:1] = value[0] + jnp.log2(value[1])
        fin[block, 1:2] = value[2] / value[1]

    def weights(kind, slot, block):
        probs = pe[kind, slot] * jnp.exp2(pair_stats[kind, slot, 0:1] - fin[block, 0:1])
        score_grad = (probs * (pd[kind, slot] - fin[block, 1:2])).astype(jnp.bfloat16)
        return probs.astype(jnp.bfloat16), score_grad

    def ret_copy(origin, slot, part, target, portion):
        return remote(
            ret_out.at[part, rows_of(portion)], ret_in.at[origin, slot, x], ret_recv.at[origin, slot],
            target, portion)

    def hold_back(slot, part, value):
        ret_out[part] = (value * scaling if slot in (DQ, DK) else value).astype(jnp.bfloat16)

    def send_back(origin, slot, part, target, value):
        hold_back(slot, part, value)
        for portion in range(HEADS):
            ret_copy(origin, slot, part, target, portion).start()

    def res_copy(slot):
        return remote(res_out.at[slot], res_in.at[slot], res_recv.at[slot], z, 1 - x)

    def send_result(slot, acc):
        value = acc[other_rows, :]
        res_out[slot] = (value * scaling if slot in (DQ, DK) else value).astype(jnp.bfloat16)
        res_copy(slot).start()

    HUB, SIDE = range(2)

    def emit(slot, *origins):
        ref, acc = ((o_ref, acc_o), (dq_ref, acc_q), (dk_ref, acc_k), (dv_ref, acc_v))[slot]
        own = acc[own_rows, :]
        own = own * scaling if slot in (DQ, DK) else own
        res_copy(slot).wait_recv()
        other = res_in[slot].astype(jnp.float32)
        for origin in origins:
            landed(ret_in.at[origin, slot], ret_recv.at[origin, slot])
            own = own + ret_in[origin, slot, x].astype(jnp.float32)
            other = other + ret_in[origin, slot, 1 - x].astype(jnp.float32)
        ref[:, own_columns] = own.astype(ref.dtype)
        ref[:, other_columns] = other.astype(ref.dtype)

    def key_side(kind, slot, block, into_v, into_k):
        probs, score_grad = weights(kind, slot, block)
        into_v[...] += dot(probs, buf[GRAD, block], 1, 0)
        into_k[...] += dot(score_grad, buf[QUERY, block], 1, 0)

    @pl.when(z == 0)
    def _():
        for array in (KEY, VALUE):
            pass_on(array)
        for array in (QUERY, GRAD):
            pass_on(array)
        own_arrives()
        limit = limits(0, 0)
        score(0, 0, 0, 0, limit)
        value = pair_stat(0, 0)
        if key_back:
            key_arrives(1)
            score(1, 0, 1, 0, limit)
            value = merge(value, pair_stat(1, 0))
        finish(0, value)
        probs, score_grad = weights(0, 0, 0)
        acc_o[...] = dot(probs, buf[VALUE, 0], 0, 0)
        acc_q[...] = dot(score_grad, buf[KEY, 0], 0, 0)
        acc_v[...] = dot(probs, buf[GRAD, 0], 1, 0)
        acc_k[...] = dot(score_grad, buf[QUERY, 0], 1, 0)
        if key_back:
            probs, score_grad = weights(1, 0, 0)
            send_back(SIDE, DV, 0, 1, dot(probs, buf[GRAD, 0], 1, 0))
            send_back(SIDE, DK, 1, 1, dot(score_grad, buf[QUERY, 0], 1, 0))
            acc_o[...] += dot(probs, buf[VALUE, 1], 0, 0)
            acc_q[...] += dot(score_grad, buf[KEY, 1], 0, 0)
        send_result(DV, acc_v)
        send_result(DK, acc_k)
        send_result(OUT, acc_o)
        send_result(DQ, acc_q)
        emit(OUT)
        emit(DQ)

    @pl.when(z == 1)
    def _():
        for array in (QUERY, GRAD, KEY, VALUE):
            pass_on(array)
        own_arrives()
        score(0, 1, 1, 1, limits(1, 0))
        key_arrives(0)
        score(1, 1, 0, 1)
        send_stat(1, merge(pair_stat(0, 1), pair_stat(1, 1)))
        all_ready()

        def scores_of(block):
            query_arrives(block)
            score(1, block, 0, block)
            score(0, block, 1, block)
            send_stat(block, merge(pair_stat(0, block), pair_stat(1, block)))

        def query_side(far, far_grad, near, near_grad):
            return (
                dot(far, buf[VALUE, 0], 0, 0) + dot(near, buf[VALUE, 1], 0, 0),
                dot(far_grad, buf[KEY, 0], 0, 0) + dot(near_grad, buf[KEY, 1], 0, 0))

        alt[...] = jnp.zeros_like(alt)

        alt[...] = jnp.zeros_like(alt)

        def finish_block(block):
            settle(block)
            far, far_grad = weights(1, block, block)
            alt[0] += dot(far, buf[GRAD, block], 1, 0)
            alt[1] += dot(far_grad, buf[QUERY, block], 1, 0)
            near, near_grad = weights(0, block, block)
            output, query_grad = query_side(far, far_grad, near, near_grad)
            hold_back(OUT, 2 * block, output)
            hold_back(DQ, 2 * block + 1, query_grad)

        pl.loop(2, last)(scores_of)
        pl.loop(2, last)(finish_block)
        scores_of(last)
        @pl.loop(2, last)
        def _(block):
            for part, slot in enumerate((OUT, DQ)):
                for portion in range(HEADS):
                    ret_copy(HUB, slot, 2 * block + part, block, portion).start()
        settle(1)
        key_side(1, 1, 1, alt.at[0], alt.at[1])
        settle(last)
        far, far_grad = weights(1, last, last)
        ret_out[0] = (alt[0] + dot(far, buf[GRAD, last], 1, 0)).astype(jnp.bfloat16)
        ret_copy(HUB, DV, 0, 0, 0).start()
        ret_out[1] = ((alt[1] + dot(far_grad, buf[QUERY, last], 1, 0)) * scaling).astype(jnp.bfloat16)
        ret_copy(HUB, DK, 1, 0, 0).start()
        ret_copy(HUB, DV, 0, 0, 1).start()
        ret_copy(HUB, DK, 1, 0, 1).start()
        near, near_grad = weights(0, last, last)
        output, query_grad = query_side(far, far_grad, near, near_grad)
        send_back(HUB, OUT, 2 * last, last, output)
        send_back(HUB, DQ, 2 * last + 1, last, query_grad)
        acc_v[...] = dot(near, buf[GRAD, last], 1, 0)
        acc_k[...] = dot(near_grad, buf[QUERY, last], 1, 0)

        far, far_grad = weights(1, 1, 1)
        near, near_grad = weights(0, 1, 1)
        acc_o[...], acc_q[...] = query_side(far, far_grad, near, near_grad)
        send_result(OUT, acc_o)
        send_result(DQ, acc_q)
        acc_v[...] += dot(near, buf[GRAD, 1], 1, 0)
        acc_k[...] += dot(near_grad, buf[QUERY, 1], 1, 0)

        @pl.loop(2, last)
        def _(block):
            key_side(0, block, block, acc_v, acc_k)
        send_result(DV, acc_v)
        send_result(DK, acc_k)

    @pl.when(z >= 2)
    def _():
        for array in (QUERY, GRAD, KEY, VALUE):
            pass_on(array)
        own_arrives()
        score(0, z, z, z, limits(z, 0))
        send_stat(z, pair_stat(0, z))

        @pl.when(ahead(z - 1))
        def _():
            query_arrives(z - 1)
            landed(ends.at[HEADS:2 * HEADS], end_recv)
            score(0, z - 1, z, z - 1, limits(z - 1, HEADS))
            send_stat(z - 1, pair_stat(0, z - 1))

        @pl.loop(z + 1, blocks)
        def _(block):
            query_arrives(block)
            score(0, block, z, block)
            send_stat(block, pair_stat(0, block))

        all_ready()
        acc_k[...] = jnp.zeros_like(acc_k)
        acc_v[...] = jnp.zeros_like(acc_v)
        @pl.when(ahead(z - 1))
        def _():
            settle(z - 1)
            probs, score_grad = weights(0, z - 1, z - 1)
            send_back(SIDE, OUT, 0, z - 1, dot(probs, buf[VALUE, z], 0, 0))
            send_back(SIDE, DQ, 1, z - 1, dot(score_grad, buf[KEY, z], 0, 0))
            acc_v[...] += dot(probs, buf[GRAD, z - 1], 1, 0)
            acc_k[...] += dot(score_grad, buf[QUERY, z - 1], 1, 0)

        @pl.loop(1, z - 1)
        def _(back):
            key_arrives(z - back)
            score(1, z - back, z - back, z)

        settle(z)
        probs, score_grad = weights(0, z, z)
        acc_v[...] += dot(probs, buf[GRAD, z], 1, 0)
        acc_k[...] += dot(score_grad, buf[QUERY, z], 1, 0)
        @pl.when(z == last)
        def _():
            send_result(DV, acc_v)
            send_result(DK, acc_k)
        acc_o[...] = dot(probs, buf[VALUE, z], 0, 0)
        acc_q[...] = dot(score_grad, buf[KEY, z], 0, 0)

        @pl.loop(1, z - 1)
        def _(back):
            block = z - back
            probs, score_grad = weights(1, block, z)
            acc_o[...] += dot(probs, buf[VALUE, block], 0, 0)
            acc_q[...] += dot(score_grad, buf[KEY, block], 0, 0)
        send_result(OUT, acc_o)
        send_result(DQ, acc_q)

        @pl.when(z < last)
        def _():
            @pl.loop(z + 1, blocks)
            def _(block):
                settle(block)
                key_side(0, block, block, acc_v, acc_k)
            send_result(DV, acc_v)
            send_result(DK, acc_k)

    @pl.when(z == 0)
    def _():
        all_ready()
    for _ in range(4):
        res_copy(0).wait_send()
        x_copy(0).wait_send()
    x_ends().wait_send()
    @pl.when(up_query)
    def _():
        for column in range(HEADS):
            up_ends(column).wait_send()
            for array in (QUERY, GRAD):
                query_copy(array, z + 1, column).wait_send()
    @pl.loop(1, z)
    def _(target):
        for _ in range(4):
            query_copy(QUERY, target, x).wait_send()
    @pl.when(down_key)
    def _():
        for _ in range(4):
            query_copy(KEY, 0, x).wait_send()
    @pl.loop(0, z + 1)
    def _(block):
        @pl.when(up_key(block))
        def _():
            for _ in range(4):
                array_copy(KEY, block, 0, z + 1).wait_send()
    @pl.when(z >= 1)
    def _():
        @pl.loop(jnp.maximum(z - 1, 1), blocks)
        def _(block):
            @pl.when((block >= z) | ahead(z - 1))
            def _():
                for target in range(1, blocks):
                    @pl.when(takes_part(block, target) & (target != z))
                    def _():
                        stat_copy(block, target).wait_send()
    @pl.when(((z == 0) & ahead(0)) | (z == 1) | ((z >= 2) & ahead(z - 1)))
    def _():
        for _ in range(4):
            ret_copy(HUB, OUT, 0, 0, 0).wait_send()
    @pl.when(z == 1)
    def _():
        @pl.loop(2, blocks)
        def _(block):
            for _ in range(4):
                ret_copy(HUB, OUT, 0, 0, 0).wait_send()

    @pl.when(z == 0)
    def _():
        emit(DV, HUB)
        emit(DK, HUB)
    @pl.when(z == 1)
    def _():
        for slot in (OUT, DQ):
            emit(slot, *((SIDE,) if query_back else ()))
        for slot in (DV, DK):
            emit(slot, *((SIDE,) if key_back else ()))
    @pl.when(z >= 2)
    def _():
        @pl.when(ahead(z))
        def _():
            emit(OUT, HUB, SIDE)
            emit(DQ, HUB, SIDE)
        @pl.when(jnp.logical_not(ahead(z)))
        def _():
            emit(OUT, HUB)
            emit(DQ, HUB)
        emit(DV)
        emit(DK)


def flush(*refs):
    sem = refs[-1]
    copies = [pltpu.make_async_copy(refs[i], refs[i + 4], sem) for i in range(4)]
    for copy in copies:
        copy.start()
    for copy in copies:
        copy.wait()


def solution(mesh):
    n = mesh.shape["ctx"]

    def local(queries, keys, values, out_grad, span_end):
        rows = queries.shape[0]
        blocks, span = n // HEADS, HEADS * rows
        f32, bf16 = jnp.float32, jnp.bfloat16
        anywhere = pl.BlockSpec(memory_space=pl.ANY)
        vmem = pl.BlockSpec(memory_space=pltpu.VMEM)
        dma = pltpu.SemaphoreType.DMA
        results = pl.pallas_call(
            functools.partial(kernel, n, rows),
            out_shape=tuple(
                pltpu.VMEM(queries.shape, kind) for kind in (bf16, f32, f32, f32)),
            in_specs=[anywhere] * 5,
            out_specs=(vmem,) * 4,
            scratch_shapes=[
                pltpu.VMEM((4, blocks, span, HEAD_DIM), bf16),
                pltpu.VMEM((2 * HEADS, 1, rows), jnp.int32),
                pltpu.VMEM((2, blocks, span, span), f32),
                pltpu.VMEM((2, blocks, span, span), f32),
                pltpu.VMEM((2, blocks, 3, span), f32),
                pltpu.VMEM((blocks, blocks, 3, span), f32),
                pltpu.VMEM((blocks, 3, span), f32),
                pltpu.VMEM((3, span), f32),
                pltpu.VMEM((blocks, 2, span), f32),
                pltpu.VMEM((span, HEAD_DIM), f32),
                pltpu.VMEM((span, HEAD_DIM), f32),
                pltpu.VMEM((span, HEAD_DIM), f32),
                pltpu.VMEM((span, HEAD_DIM), f32),
                pltpu.VMEM((2, span, HEAD_DIM), f32),
                pltpu.VMEM((2 * blocks, span, HEAD_DIM), bf16),
                pltpu.VMEM((2, 4, HEADS, rows, HEAD_DIM), bf16),
                pltpu.VMEM((4, rows, HEAD_DIM), bf16),
                pltpu.VMEM((4, rows, HEAD_DIM), bf16),
                dma((2,)),
                dma((5,)),
                dma((2, blocks)),
                dma,
                dma((blocks - 1, blocks - 1)),
                dma((2, 4)),
                dma((4,)),
                dma,
                pltpu.SemaphoreType.REGULAR((blocks - 1,)),
            ],
            compiler_params=pltpu.CompilerParams(collective_id=0, has_side_effects=True),
        )(queries, keys, values, out_grad, span_end[None])
        return pl.pallas_call(
            flush,
            out_shape=tuple(
                jax.ShapeDtypeStruct(queries.shape, kind) for kind in (bf16, f32, f32, f32)),
            in_specs=[vmem] * 4,
            out_specs=(anywhere,) * 4,
            scratch_shapes=[dma],
        )(*(pltpu.with_memory_space_constraint(result, pltpu.VMEM) for result in results))

    spec = P(("dp", "ctx"), None)
    return jax.shard_map(
        local, mesh=mesh, in_specs=(spec,) * 4 + (P(("dp", "ctx")),),
        out_specs=(spec,) * 4, check_vma=False)
```

```python
import functools
import math

import jax
import jax.numpy as jnp
from jax import lax
from jax.experimental import pallas as pl
from jax.experimental.pallas import tpu as pltpu
from jax.sharding import PartitionSpec as P

HEADS = 2
HEAD_DIM = 128
IMG = 288
HIDDEN = -1e30
KEY, VALUE, QUERY, GRAD = range(4)


def dot(a, b, a_dim, b_dim):
    return lax.dot_general(a, b, (((a_dim,), (b_dim,)), ((), ())), preferred_element_type=jnp.float32)


def kernel(
    n, rows,
    q_in, k_in, v_in, g_in, ends_in,
    o_ref, dq_ref, dk_ref, dv_ref,
    buf, ends, pe, pd, pair_stats, st_in, st_out, total, fin,
    acc_o, acc_q, acc_k, acc_v, alt, ret_out, ret_in, res_out, res_in,
    local_sem, x_recv, z_recv, end_recv, st_recv, ret_recv, res_recv, sent, ready,
):
    scaling = HEAD_DIM ** -0.5
    binary = scaling / math.log(2.0)
    blocks = n // HEADS
    span = HEADS * rows
    cut = blocks * span - IMG
    last = blocks - 1
    me = lax.axis_index("ctx")
    z = me // HEADS
    x = me % HEADS
    sources = (k_in, v_in, q_in, g_in)
    OUT, DQ, DK, DV = range(4)
    HUB, SIDE = range(2)

    def device(block, column):
        return {"ctx": block * HEADS + column}

    def ahead(block):
        return ((block + 1) * span < cut) & (block + 1 < blocks)

    def rows_of(portion):
        return pl.ds(pl.multiple_of(portion * rows, 16), rows)

    def columns_of(head):
        return pl.ds(pl.multiple_of(head * HEAD_DIM, HEAD_DIM), HEAD_DIM)

    own_rows, other_rows = rows_of(x), rows_of(1 - x)
    own_columns, other_columns = columns_of(x), columns_of(1 - x)

    key_back = span < cut
    query_back = 2 * span < cut and last > 1
    down_key = (z == 1) & ahead(0)
    up_query = (z >= 1) & ahead(z)

    def up_key(block):
        return (z < last) & ((z == 0) | (block >= 2))

    def takes_part(block, target):
        return (target >= 1) & ((target <= block) | ((target == block + 1) & ahead(block)))

    barrier = pltpu.get_barrier_semaphore()
    for target in range(1, blocks):
        @pl.when(target > z)
        def _():
            for column in range(HEADS):
                pl.semaphore_signal(barrier, inc=1, device_id=device(target, column))
    pl.semaphore_signal(barrier, inc=1, device_id=device(z, 1 - x))

    def own_copy(array):
        return pltpu.make_async_copy(
            sources[array].at[:, own_columns], buf.at[array, z, own_rows], local_sem.at[0])

    for array in range(4):
        own_copy(array).start()
    pltpu.make_async_copy(ends_in, ends.at[x], local_sem.at[1]).start()

    pl.semaphore_wait(barrier, HEADS * z + 1)
    for target in range(last):
        @pl.when(target < z)
        def _():
            for column in range(HEADS):
                pl.semaphore_signal(ready.at[z - 1], inc=1, device_id=device(target, column))

    def remote(src, dst, recv, target, column):
        return pltpu.make_async_remote_copy(
            src_ref=src, dst_ref=dst, send_sem=sent, recv_sem=recv, device_id=device(target, column))

    def array_copy(array, block, portion, target, own=False):
        dst = buf.at[array, block, rows_of(portion)]
        return remote(
            sources[array].at[:, own_columns] if own else dst, dst,
            z_recv.at[array // 2, block], target, x)

    def query_copy(array, target, column):
        return remote(
            sources[array].at[:, columns_of(column)], buf.at[array, z, own_rows],
            z_recv.at[array // 2, z], target, column)

    def x_copy(array):
        return remote(
            sources[array].at[:, other_columns], buf.at[array, z, own_rows], x_recv.at[array], z, 1 - x)

    def x_ends():
        return remote(ends_in, ends.at[x], x_recv.at[4], z, 1 - x)

    def up_ends(column):
        return remote(ends_in, ends.at[HEADS + x], end_recv, z + 1, column)

    def landed(ref, sem):
        pltpu.make_async_copy(ref, ref, sem).wait()

    def send_query(target):
        for column in (x, 1 - x):
            for array in (QUERY, GRAD):
                query_copy(array, target, column).start()

    def send_key(array, portion, own):
        @pl.when(up_key(z))
        def _():
            array_copy(array, z, portion, z + 1, own).start()

    @pl.when(z == 0)
    def _():
        for array in (KEY, VALUE, QUERY, GRAD):
            x_copy(array).start()
    @pl.when(z > 0)
    def _():
        for array in (QUERY, GRAD, KEY, VALUE):
            x_copy(array).start()
    for target in range(last - 1, 0, -1):
        @pl.when((target < z) & (z > 2))
        def _():
            for array in (QUERY, GRAD):
                query_copy(array, target, x).start()
    @pl.when(z == 2)
    def _():
        send_query(1)
    @pl.when(down_key)
    def _():
        for column in (x, 1 - x):
            for array in (KEY, VALUE):
                query_copy(array, 0, column).start()
    x_ends().start()

    @pl.when(z < last)
    def _():
        pl.semaphore_wait(ready.at[z], HEADS)
    for target in range(2, blocks):
        @pl.when(up_query & (target == z + 1))
        def _():
            for column in range(HEADS):
                up_ends(column).start()
            for array in (QUERY, GRAD):
                query_copy(array, target, x).start()
    @pl.when(z == 0)
    def _():
        for array in (KEY, VALUE):
            send_key(array, x, True)

    def all_ready():
        @pl.loop(z + 2, blocks)
        def _(target):
            pl.semaphore_wait(ready.at[target - 1], HEADS)

    def pass_on(array):
        landed(buf.at[array, z, other_rows], x_recv.at[array])
        if array in (KEY, VALUE):
            @pl.when(z > 0)
            def _():
                send_key(array, x, True)
            send_key(array, 1 - x, False)
        else:
            @pl.when(up_query)
            def _():
                array_copy(array, z, 1 - x, z + 1).start()
            @pl.when(z > 2)
            def _():
                array_copy(array, z, 1 - x, z - 1).start()
                if array == GRAD:
                    for target in range(last - 2, 0, -1):
                        @pl.when(target < z - 1)
                        def _():
                            for half in (QUERY, GRAD):
                                array_copy(half, z, 1 - x, target).start()

    def key_arrives(block):
        landed(buf.at[KEY:VALUE + 1, block], z_recv.at[0, block])
        @pl.when(up_key(block) & (block < z))
        def _():
            for array in (KEY, VALUE):
                for portion in range(HEADS):
                    array_copy(array, block, portion, z + 1).start()

    def query_arrives(block):
        landed(buf.at[QUERY:GRAD + 1, block], z_recv.at[1, block])

    def own_arrives():
        landed(buf.at[:, z, own_rows], local_sem.at[0])
        landed(ends.at[x], local_sem.at[1])
        landed(ends.at[1 - x], x_recv.at[4])

    def limits(block, slot):
        joined = jnp.concatenate([ends[slot + portion] for portion in range(HEADS)], axis=1)
        position = lax.broadcasted_iota(jnp.int32, (1, span), 1) + block * span
        return jnp.maximum(position + 1, joined)

    key_row = lax.broadcasted_iota(jnp.int32, (span, span), 0)

    def score(kind, slot, key_block, query_block, limit=None):
        scores = dot(buf[KEY, key_block], buf[QUERY, query_block], 1, 1)
        prob_grad = dot(buf[VALUE, key_block], buf[GRAD, query_block], 1, 1)
        if limit is not None:
            scores = jnp.where(key_row + key_block * span < limit, scores, HIDDEN)
        highest = jnp.max(scores, axis=0, keepdims=True)
        probs = jnp.exp2((scores - highest) * binary)
        pe[kind, slot] = probs
        pd[kind, slot] = prob_grad
        pair_stats[kind, slot, 0:1] = highest * binary
        pair_stats[kind, slot, 1:2] = jnp.sum(probs, axis=0, keepdims=True)
        pair_stats[kind, slot, 2:3] = jnp.sum(probs * prob_grad, axis=0, keepdims=True)

    def stat(ref):
        return ref[0:1], ref[1:2], ref[2:3]

    def pair_stat(kind, slot):
        return stat(pair_stats.at[kind, slot])

    def keep(ref, value):
        for row in range(3):
            ref[row:row + 1] = value[row]

    def merge(a, b):
        highest = jnp.maximum(a[0], b[0])
        fa, fb = jnp.exp2(a[0] - highest), jnp.exp2(b[0] - highest)
        return highest, a[1] * fa + b[1] * fb, a[2] * fa + b[2] * fb

    def stat_copy(block, target):
        return remote(st_out.at[block], st_in.at[z, block], st_recv.at[z - 1, block - 1], target, x)

    def send_stat(block, value):
        keep(st_out.at[block], value)
        for target in range(1, blocks):
            @pl.when(takes_part(block, target) & (target != z))
            def _():
                stat_copy(block, target).start()

    def settle(block):
        keep(total, stat(st_out.at[block]))
        for source in range(1, blocks):
            @pl.when(takes_part(block, source) & (source != z))
            def _():
                landed(st_in.at[source, block], st_recv.at[source - 1, block - 1])
                keep(total, merge(stat(total), stat(st_in.at[source, block])))
        finish(block, stat(total))

    def finish(block, value):
        fin[block, 0:1] = value[0] + jnp.log2(value[1])
        fin[block, 1:2] = value[2] / value[1]

    def weights(kind, slot, block):
        probs = pe[kind, slot] * jnp.exp2(pair_stats[kind, slot, 0:1] - fin[block, 0:1])
        score_grad = (probs * (pd[kind, slot] - fin[block, 1:2])).astype(jnp.bfloat16)
        return probs.astype(jnp.bfloat16), score_grad

    def ret_index(origin, slot):
        return slot + 4 if origin == SIDE and slot in (OUT, DQ) else slot

    def ret_copy(origin, slot, part, target, portion):
        return remote(
            ret_out.at[part, rows_of(portion)], ret_in.at[origin, slot, x], ret_recv.at[ret_index(origin, slot)],
            target, portion)

    def hold_back(slot, part, value):
        ret_out[part] = (value * scaling if slot in (DQ, DK) else value).astype(jnp.bfloat16)

    def send_back(origin, slot, part, target, value):
        hold_back(slot, part, value)
        for portion in range(HEADS):
            ret_copy(origin, slot, part, target, portion).start()

    def res_copy(slot):
        return remote(res_out.at[slot], res_in.at[slot], res_recv.at[slot], z, 1 - x)

    def send_result(slot, acc):
        value = acc[other_rows, :]
        res_out[slot] = (value * scaling if slot in (DQ, DK) else value).astype(jnp.bfloat16)
        res_copy(slot).start()


    def emit(slot, *origins):
        ref, acc = ((o_ref, acc_o), (dq_ref, acc_q), (dk_ref, acc_k), (dv_ref, acc_v))[slot]
        own = acc[own_rows, :]
        own = own * scaling if slot in (DQ, DK) else own
        res_copy(slot).wait_recv()
        other = res_in[slot].astype(jnp.float32)
        for origin in origins:
            landed(ret_in.at[origin, slot], ret_recv.at[ret_index(origin, slot)])
            own = own + ret_in[origin, slot, x].astype(jnp.float32)
            other = other + ret_in[origin, slot, 1 - x].astype(jnp.float32)
        ref[:, own_columns] = own.astype(ref.dtype)
        ref[:, other_columns] = other.astype(ref.dtype)

    def key_side(kind, slot, block, into_v, into_k):
        probs, score_grad = weights(kind, slot, block)
        into_v[...] += dot(probs, buf[GRAD, block], 1, 0)
        into_k[...] += dot(score_grad, buf[QUERY, block], 1, 0)

    @pl.when(z == 0)
    def _():
        for array in (KEY, VALUE):
            pass_on(array)
        for array in (QUERY, GRAD):
            pass_on(array)
        own_arrives()
        limit = limits(0, 0)
        score(0, 0, 0, 0, limit)
        value = pair_stat(0, 0)
        if key_back:
            key_arrives(1)
            score(1, 0, 1, 0, limit)
            value = merge(value, pair_stat(1, 0))
        finish(0, value)
        probs, score_grad = weights(0, 0, 0)
        acc_o[...] = dot(probs, buf[VALUE, 0], 0, 0)
        acc_q[...] = dot(score_grad, buf[KEY, 0], 0, 0)
        acc_v[...] = dot(probs, buf[GRAD, 0], 1, 0)
        acc_k[...] = dot(score_grad, buf[QUERY, 0], 1, 0)
        if key_back:
            probs, score_grad = weights(1, 0, 0)
            send_back(SIDE, DV, 0, 1, dot(probs, buf[GRAD, 0], 1, 0))
            send_back(SIDE, DK, 1, 1, dot(score_grad, buf[QUERY, 0], 1, 0))
            acc_o[...] += dot(probs, buf[VALUE, 1], 0, 0)
            acc_q[...] += dot(score_grad, buf[KEY, 1], 0, 0)
        send_result(DV, acc_v)
        send_result(DK, acc_k)
        send_result(OUT, acc_o)
        send_result(DQ, acc_q)
        emit(OUT)
        emit(DQ)

    @pl.when(z == 1)
    def _():
        for array in (QUERY, GRAD, KEY, VALUE):
            pass_on(array)
        own_arrives()
        score(0, 1, 1, 1, limits(1, 0))
        key_arrives(0)
        score(1, 1, 0, 1)
        send_stat(1, merge(pair_stat(0, 1), pair_stat(1, 1)))
        all_ready()

        def scores_of(block):
            query_arrives(block)
            score(1, block, 0, block)
            score(0, block, 1, block)
            send_stat(block, merge(pair_stat(0, block), pair_stat(1, block)))

        def query_side(far, far_grad, near, near_grad):
            return (
                dot(far, buf[VALUE, 0], 0, 0) + dot(near, buf[VALUE, 1], 0, 0),
                dot(far_grad, buf[KEY, 0], 0, 0) + dot(near_grad, buf[KEY, 1], 0, 0))

        alt[...] = jnp.zeros_like(alt)

        alt[...] = jnp.zeros_like(alt)

        def finish_block(block):
            settle(block)
            far, far_grad = weights(1, block, block)
            alt[0] += dot(far, buf[GRAD, block], 1, 0)
            alt[1] += dot(far_grad, buf[QUERY, block], 1, 0)
            near, near_grad = weights(0, block, block)
            output, query_grad = query_side(far, far_grad, near, near_grad)
            hold_back(OUT, 2 * block, output)
            hold_back(DQ, 2 * block + 1, query_grad)

        pl.loop(2, last)(scores_of)
        pl.loop(2, last)(finish_block)
        scores_of(last)
        @pl.loop(2, last)
        def _(block):
            for part, slot in enumerate((OUT, DQ)):
                for portion in range(HEADS):
                    ret_copy(HUB, slot, 2 * block + part, block, portion).start()
        settle(1)
        key_side(1, 1, 1, alt.at[0], alt.at[1])
        settle(last)
        far, far_grad = weights(1, last, last)
        ret_out[0] = (alt[0] + dot(far, buf[GRAD, last], 1, 0)).astype(jnp.bfloat16)
        ret_copy(HUB, DV, 0, 0, 0).start()
        ret_out[1] = ((alt[1] + dot(far_grad, buf[QUERY, last], 1, 0)) * scaling).astype(jnp.bfloat16)
        ret_copy(HUB, DK, 1, 0, 0).start()
        ret_copy(HUB, DV, 0, 0, 1).start()
        ret_copy(HUB, DK, 1, 0, 1).start()
        near, near_grad = weights(0, last, last)
        output, query_grad = query_side(far, far_grad, near, near_grad)
        send_back(HUB, OUT, 2 * last, last, output)
        send_back(HUB, DQ, 2 * last + 1, last, query_grad)
        acc_v[...] = dot(near, buf[GRAD, last], 1, 0)
        acc_k[...] = dot(near_grad, buf[QUERY, last], 1, 0)

        far, far_grad = weights(1, 1, 1)
        near, near_grad = weights(0, 1, 1)
        acc_o[...], acc_q[...] = query_side(far, far_grad, near, near_grad)
        send_result(OUT, acc_o)
        send_result(DQ, acc_q)
        acc_v[...] += dot(near, buf[GRAD, 1], 1, 0)
        acc_k[...] += dot(near_grad, buf[QUERY, 1], 1, 0)

        @pl.loop(2, last)
        def _(block):
            key_side(0, block, block, acc_v, acc_k)
        send_result(DV, acc_v)
        send_result(DK, acc_k)

    @pl.when(z >= 2)
    def _():
        for array in (QUERY, GRAD, KEY, VALUE):
            pass_on(array)
        own_arrives()
        score(0, z, z, z, limits(z, 0))
        send_stat(z, pair_stat(0, z))

        @pl.when(ahead(z - 1))
        def _():
            query_arrives(z - 1)
            landed(ends.at[HEADS:2 * HEADS], end_recv)
            score(0, z - 1, z, z - 1, limits(z - 1, HEADS))
            send_stat(z - 1, pair_stat(0, z - 1))

        @pl.loop(z + 1, blocks)
        def _(block):
            query_arrives(block)
            score(0, block, z, block)
            send_stat(block, pair_stat(0, block))

        all_ready()
        acc_k[...] = jnp.zeros_like(acc_k)
        acc_v[...] = jnp.zeros_like(acc_v)
        @pl.when(ahead(z - 1))
        def _():
            settle(z - 1)
            probs, score_grad = weights(0, z - 1, z - 1)
            send_back(SIDE, OUT, 0, z - 1, dot(probs, buf[VALUE, z], 0, 0))
            send_back(SIDE, DQ, 1, z - 1, dot(score_grad, buf[KEY, z], 0, 0))
            acc_v[...] += dot(probs, buf[GRAD, z - 1], 1, 0)
            acc_k[...] += dot(score_grad, buf[QUERY, z - 1], 1, 0)

        @pl.loop(1, z - 1)
        def _(back):
            key_arrives(z - back)
            score(1, z - back, z - back, z)

        settle(z)
        probs, score_grad = weights(0, z, z)
        acc_v[...] += dot(probs, buf[GRAD, z], 1, 0)
        acc_k[...] += dot(score_grad, buf[QUERY, z], 1, 0)
        @pl.when(z == last)
        def _():
            send_result(DV, acc_v)
            send_result(DK, acc_k)
        acc_o[...] = dot(probs, buf[VALUE, z], 0, 0)
        acc_q[...] = dot(score_grad, buf[KEY, z], 0, 0)

        @pl.loop(1, z - 1)
        def _(back):
            block = z - back
            probs, score_grad = weights(1, block, z)
            acc_o[...] += dot(probs, buf[VALUE, block], 0, 0)
            acc_q[...] += dot(score_grad, buf[KEY, block], 0, 0)
        send_result(OUT, acc_o)
        send_result(DQ, acc_q)

        @pl.when(z < last)
        def _():
            @pl.loop(z + 1, blocks)
            def _(block):
                settle(block)
                key_side(0, block, block, acc_v, acc_k)
            send_result(DV, acc_v)
            send_result(DK, acc_k)

    @pl.when(z == 0)
    def _():
        all_ready()
    for _ in range(4):
        res_copy(0).wait_send()
        x_copy(0).wait_send()
    x_ends().wait_send()
    @pl.when(up_query)
    def _():
        for column in range(HEADS):
            up_ends(column).wait_send()
            for array in (QUERY, GRAD):
                query_copy(array, z + 1, column).wait_send()
    @pl.loop(1, z)
    def _(target):
        for _ in range(4):
            query_copy(QUERY, target, x).wait_send()
    @pl.when(down_key)
    def _():
        for _ in range(4):
            query_copy(KEY, 0, x).wait_send()
    @pl.loop(0, z + 1)
    def _(block):
        @pl.when(up_key(block))
        def _():
            for _ in range(4):
                array_copy(KEY, block, 0, z + 1).wait_send()
    @pl.when(z >= 1)
    def _():
        @pl.loop(jnp.maximum(z - 1, 1), blocks)
        def _(block):
            @pl.when((block >= z) | ahead(z - 1))
            def _():
                for target in range(1, blocks):
                    @pl.when(takes_part(block, target) & (target != z))
                    def _():
                        stat_copy(block, target).wait_send()
    @pl.when(((z == 0) & ahead(0)) | (z == 1) | ((z >= 2) & ahead(z - 1)))
    def _():
        for _ in range(4):
            ret_copy(HUB, OUT, 0, 0, 0).wait_send()
    @pl.when(z == 1)
    def _():
        @pl.loop(2, blocks)
        def _(block):
            for _ in range(4):
                ret_copy(HUB, OUT, 0, 0, 0).wait_send()

    @pl.when(z == 0)
    def _():
        emit(DV, HUB)
        emit(DK, HUB)
    @pl.when(z == 1)
    def _():
        for slot in (OUT, DQ):
            emit(slot, *((SIDE,) if query_back else ()))
        for slot in (DV, DK):
            emit(slot, *((SIDE,) if key_back else ()))
    @pl.when(z >= 2)
    def _():
        @pl.when(z == last)
        def _():
            emit(DV)
            emit(DK)
        @pl.when(ahead(z))
        def _():
            emit(OUT, HUB, SIDE)
            emit(DQ, HUB, SIDE)
        @pl.when(jnp.logical_not(ahead(z)))
        def _():
            emit(OUT, HUB)
            emit(DQ, HUB)
        @pl.when(z < last)
        def _():
            emit(DV)
            emit(DK)


def flush(*refs):
    sem = refs[-1]
    copies = [pltpu.make_async_copy(refs[i], refs[i + 4], sem) for i in range(4)]
    for copy in copies:
        copy.start()
    for copy in copies:
        copy.wait()


def solution(mesh):
    n = mesh.shape["ctx"]

    def local(queries, keys, values, out_grad, span_end):
        rows = queries.shape[0]
        blocks, span = n // HEADS, HEADS * rows
        f32, bf16 = jnp.float32, jnp.bfloat16
        anywhere = pl.BlockSpec(memory_space=pl.ANY)
        vmem = pl.BlockSpec(memory_space=pltpu.VMEM)
        dma = pltpu.SemaphoreType.DMA
        results = pl.pallas_call(
            functools.partial(kernel, n, rows),
            out_shape=tuple(
                pltpu.VMEM(queries.shape, kind) for kind in (bf16, f32, f32, f32)),
            in_specs=[anywhere] * 5,
            out_specs=(vmem,) * 4,
            scratch_shapes=[
                pltpu.VMEM((4, blocks, span, HEAD_DIM), bf16),
                pltpu.VMEM((2 * HEADS, 1, rows), jnp.int32),
                pltpu.VMEM((2, blocks, span, span), f32),
                pltpu.VMEM((2, blocks, span, span), f32),
                pltpu.VMEM((2, blocks, 3, span), f32),
                pltpu.VMEM((blocks, blocks, 3, span), f32),
                pltpu.VMEM((blocks, 3, span), f32),
                pltpu.VMEM((3, span), f32),
                pltpu.VMEM((blocks, 2, span), f32),
                pltpu.VMEM((span, HEAD_DIM), f32),
                pltpu.VMEM((span, HEAD_DIM), f32),
                pltpu.VMEM((span, HEAD_DIM), f32),
                pltpu.VMEM((span, HEAD_DIM), f32),
                pltpu.VMEM((2, span, HEAD_DIM), f32),
                pltpu.VMEM((2 * blocks, span, HEAD_DIM), bf16),
                pltpu.VMEM((2, 4, HEADS, rows, HEAD_DIM), bf16),
                pltpu.VMEM((4, rows, HEAD_DIM), bf16),
                pltpu.VMEM((4, rows, HEAD_DIM), bf16),
                dma((2,)),
                dma((5,)),
                dma((2, blocks)),
                dma,
                dma((blocks - 1, blocks - 1)),
                dma((6,)),
                dma((4,)),
                dma,
                pltpu.SemaphoreType.REGULAR((blocks - 1,)),
            ],
            compiler_params=pltpu.CompilerParams(
                collective_id=0, has_side_effects=True),
        )(queries, keys, values, out_grad, span_end[None])
        return pl.pallas_call(
            flush,
            out_shape=tuple(
                jax.ShapeDtypeStruct(queries.shape, kind) for kind in (bf16, f32, f32, f32)),
            in_specs=[vmem] * 4,
            out_specs=(anywhere,) * 4,
            scratch_shapes=[dma],
        )(*(pltpu.with_memory_space_constraint(result, pltpu.VMEM) for result in results))

    spec = P(("dp", "ctx"), None)
    return jax.shard_map(
        local, mesh=mesh, in_specs=(spec,) * 4 + (P(("dp", "ctx")),),
        out_specs=(spec,) * 4, check_vma=False)
```

```python
import functools
import math

import jax
import jax.numpy as jnp
from jax import lax
from jax.experimental import pallas as pl
from jax.experimental.pallas import tpu as pltpu
from jax.sharding import PartitionSpec as P

HEADS = 2
HEAD_DIM = 128
IMG = 288
HIDDEN = -1e30
KEY, VALUE, QUERY, GRAD = range(4)


def dot(a, b, a_dim, b_dim):
    return lax.dot_general(a, b, (((a_dim,), (b_dim,)), ((), ())), preferred_element_type=jnp.float32)


def kernel(
    n, rows,
    q_in, k_in, v_in, g_in, ends_in,
    o_ref, dq_ref, dk_ref, dv_ref,
    buf, ends, pe, pd, pair_stats, st_in, st_out, total, fin,
    acc_o, acc_q, acc_k, acc_v, alt, ret_out, ret_in, res_out, res_in,
    local_sem, x_recv, z_recv, end_recv, st_recv, ret_recv, res_recv, sent, ready,
):
    scaling = HEAD_DIM ** -0.5
    binary = scaling / math.log(2.0)
    blocks = n // HEADS
    span = HEADS * rows
    cut = blocks * span - IMG
    last = blocks - 1
    me = lax.axis_index("ctx")
    z = me // HEADS
    x = me % HEADS
    sources = (k_in, v_in, q_in, g_in)
    OUT, DQ, DK, DV = range(4)

    def device(block, column):
        return {"ctx": block * HEADS + column}

    def ahead(block):
        return ((block + 1) * span < cut) & (block + 1 < blocks)

    def rows_of(portion):
        return pl.ds(pl.multiple_of(portion * rows, 16), rows)

    def columns_of(head):
        return pl.ds(pl.multiple_of(head * HEAD_DIM, HEAD_DIM), HEAD_DIM)

    own_rows, other_rows = rows_of(x), rows_of(1 - x)
    own_columns, other_columns = columns_of(x), columns_of(1 - x)

    key_back = span < cut
    query_back = 2 * span < cut and last > 1
    down_key = (z == 1) & ahead(0)
    up_query = (z >= 1) & ahead(z)

    def up_key(block):
        return (z < last) & ((z == 0) | (block >= 2))

    def takes_part(block, target):
        return (target >= 1) & ((target <= block) | ((target == block + 1) & ahead(block)))

    barrier = pltpu.get_barrier_semaphore()
    for target in range(1, blocks):
        @pl.when(target > z)
        def _():
            for column in range(HEADS):
                pl.semaphore_signal(barrier, inc=1, device_id=device(target, column))
    pl.semaphore_signal(barrier, inc=1, device_id=device(z, 1 - x))

    def own_copy(array):
        return pltpu.make_async_copy(
            sources[array].at[:, own_columns], buf.at[array, z, own_rows], local_sem.at[0])

    for array in range(4):
        own_copy(array).start()
    pltpu.make_async_copy(ends_in, ends.at[x], local_sem.at[1]).start()

    pl.semaphore_wait(barrier, HEADS * z + 1)
    for target in range(last):
        @pl.when(target < z)
        def _():
            for column in range(HEADS):
                pl.semaphore_signal(ready.at[z - 1], inc=1, device_id=device(target, column))

    def remote(src, dst, recv, target, column):
        return pltpu.make_async_remote_copy(
            src_ref=src, dst_ref=dst, send_sem=sent, recv_sem=recv, device_id=device(target, column))

    def array_copy(array, block, portion, target, own=False):
        dst = buf.at[array, block, rows_of(portion)]
        return remote(
            sources[array].at[:, own_columns] if own else dst, dst,
            z_recv.at[array // 2, block], target, x)

    def query_copy(array, target, column):
        return remote(
            sources[array].at[:, columns_of(column)], buf.at[array, z, own_rows],
            z_recv.at[array // 2, z], target, column)

    def x_copy(array):
        return remote(
            sources[array].at[:, other_columns], buf.at[array, z, own_rows], x_recv.at[array], z, 1 - x)

    def x_ends():
        return remote(ends_in, ends.at[x], x_recv.at[4], z, 1 - x)

    def up_ends(column):
        return remote(ends_in, ends.at[HEADS + x], end_recv, z + 1, column)

    def landed(ref, sem):
        pltpu.make_async_copy(ref, ref, sem).wait()

    def send_query(target):
        for column in (x, 1 - x):
            for array in (QUERY, GRAD):
                query_copy(array, target, column).start()

    def send_key(array, portion, own):
        @pl.when(up_key(z))
        def _():
            array_copy(array, z, portion, z + 1, own).start()

    @pl.when(z == 0)
    def _():
        for array in (KEY, VALUE, QUERY, GRAD):
            x_copy(array).start()
    @pl.when(z > 0)
    def _():
        for array in (QUERY, GRAD, KEY, VALUE):
            x_copy(array).start()
    for target in range(last - 1, 0, -1):
        @pl.when((target < z) & (z > 2))
        def _():
            for array in (QUERY, GRAD):
                query_copy(array, target, x).start()
    @pl.when(z == 2)
    def _():
        send_query(1)
    @pl.when(down_key)
    def _():
        for column in (x, 1 - x):
            for array in (KEY, VALUE):
                query_copy(array, 0, column).start()
    x_ends().start()

    @pl.when(z < last)
    def _():
        pl.semaphore_wait(ready.at[z], HEADS)
    for target in range(2, blocks):
        @pl.when(up_query & (target == z + 1))
        def _():
            for column in range(HEADS):
                up_ends(column).start()
            for array in (QUERY, GRAD):
                query_copy(array, target, x).start()
    @pl.when(z == 0)
    def _():
        for array in (KEY, VALUE):
            send_key(array, x, True)

    def all_ready():
        @pl.loop(z + 2, blocks)
        def _(target):
            pl.semaphore_wait(ready.at[target - 1], HEADS)

    def pass_on(array):
        landed(buf.at[array, z, other_rows], x_recv.at[array])
        if array in (KEY, VALUE):
            @pl.when(z > 0)
            def _():
                send_key(array, x, True)
            send_key(array, 1 - x, False)
        else:
            @pl.when(up_query)
            def _():
                array_copy(array, z, 1 - x, z + 1).start()
            @pl.when(z > 2)
            def _():
                array_copy(array, z, 1 - x, z - 1).start()
                if array == GRAD:
                    for target in range(last - 2, 0, -1):
                        @pl.when(target < z - 1)
                        def _():
                            for half in (QUERY, GRAD):
                                array_copy(half, z, 1 - x, target).start()

    def key_arrives(block):
        landed(buf.at[KEY:VALUE + 1, block], z_recv.at[0, block])
        @pl.when(up_key(block) & (block < z))
        def _():
            for array in (KEY, VALUE):
                for portion in range(HEADS):
                    array_copy(array, block, portion, z + 1).start()

    def query_arrives(block):
        landed(buf.at[QUERY:GRAD + 1, block], z_recv.at[1, block])

    def own_arrives():
        landed(buf.at[:, z, own_rows], local_sem.at[0])
        landed(ends.at[x], local_sem.at[1])
        landed(ends.at[1 - x], x_recv.at[4])

    def limits(block, slot):
        joined = jnp.concatenate([ends[slot + portion] for portion in range(HEADS)], axis=1)
        position = lax.broadcasted_iota(jnp.int32, (1, span), 1) + block * span
        return jnp.maximum(position + 1, joined)

    key_row = lax.broadcasted_iota(jnp.int32, (span, span), 0)

    def score(kind, slot, key_block, query_block, limit=None):
        scores = dot(buf[KEY, key_block], buf[QUERY, query_block], 1, 1)
        prob_grad = dot(buf[VALUE, key_block], buf[GRAD, query_block], 1, 1)
        if limit is not None:
            scores = jnp.where(key_row + key_block * span < limit, scores, HIDDEN)
        highest = jnp.max(scores, axis=0, keepdims=True)
        probs = jnp.exp2((scores - highest) * binary)
        pe[kind, slot] = probs
        pd[kind, slot] = prob_grad
        pair_stats[kind, slot, 0:1] = highest * binary
        pair_stats[kind, slot, 1:2] = jnp.sum(probs, axis=0, keepdims=True)
        pair_stats[kind, slot, 2:3] = jnp.sum(probs * prob_grad, axis=0, keepdims=True)

    def stat(ref):
        return ref[0:1], ref[1:2], ref[2:3]

    def pair_stat(kind, slot):
        return stat(pair_stats.at[kind, slot])

    def keep(ref, value):
        for row in range(3):
            ref[row:row + 1] = value[row]

    def merge(a, b):
        highest = jnp.maximum(a[0], b[0])
        fa, fb = jnp.exp2(a[0] - highest), jnp.exp2(b[0] - highest)
        return highest, a[1] * fa + b[1] * fb, a[2] * fa + b[2] * fb

    def stat_copy(block, target):
        return remote(st_out.at[block], st_in.at[z, block], st_recv.at[z - 1, block - 1], target, x)

    def send_stat(block, value):
        keep(st_out.at[block], value)
        for target in range(1, blocks):
            @pl.when(takes_part(block, target) & (target != z))
            def _():
                stat_copy(block, target).start()

    def settle(block):
        keep(total, stat(st_out.at[block]))
        for source in range(1, blocks):
            @pl.when(takes_part(block, source) & (source != z))
            def _():
                landed(st_in.at[source, block], st_recv.at[source - 1, block - 1])
                keep(total, merge(stat(total), stat(st_in.at[source, block])))
        finish(block, stat(total))

    def finish(block, value):
        fin[block, 0:1] = value[0] + jnp.log2(value[1])
        fin[block, 1:2] = value[2] / value[1]

    def weights(kind, slot, block):
        probs = pe[kind, slot] * jnp.exp2(pair_stats[kind, slot, 0:1] - fin[block, 0:1])
        score_grad = (probs * (pd[kind, slot] - fin[block, 1:2])).astype(jnp.bfloat16)
        return probs.astype(jnp.bfloat16), score_grad

    def ret_copy(origin, slot, part, target, portion):
        return remote(
            ret_out.at[part, rows_of(portion)], ret_in.at[origin, slot, x], ret_recv.at[origin, slot],
            target, portion)

    def hold_back(slot, part, value):
        ret_out[part] = (value * scaling if slot in (DQ, DK) else value).astype(jnp.bfloat16)

    def send_back(origin, slot, part, target, value):
        hold_back(slot, part, value)
        for portion in range(HEADS):
            ret_copy(origin, slot, part, target, portion).start()

    def res_copy(slot):
        return remote(res_out.at[slot], res_in.at[slot], res_recv.at[slot], z, 1 - x)

    def send_result(slot, acc):
        value = acc[other_rows, :]
        res_out[slot] = (value * scaling if slot in (DQ, DK) else value).astype(jnp.bfloat16)
        res_copy(slot).start()

    HUB, SIDE = range(2)

    def emit(slot, *origins):
        ref, acc = ((o_ref, acc_o), (dq_ref, acc_q), (dk_ref, acc_k), (dv_ref, acc_v))[slot]
        own = acc[own_rows, :]
        own = own * scaling if slot in (DQ, DK) else own
        res_copy(slot).wait_recv()
        other = res_in[slot].astype(jnp.float32)
        for origin in origins:
            landed(ret_in.at[origin, slot], ret_recv.at[origin, slot])
            own = own + ret_in[origin, slot, x].astype(jnp.float32)
            other = other + ret_in[origin, slot, 1 - x].astype(jnp.float32)
        ref[:, own_columns] = own.astype(ref.dtype)
        ref[:, other_columns] = other.astype(ref.dtype)

    def key_side(kind, slot, block, into_v, into_k):
        probs, score_grad = weights(kind, slot, block)
        into_v[...] += dot(probs, buf[GRAD, block], 1, 0)
        into_k[...] += dot(score_grad, buf[QUERY, block], 1, 0)

    @pl.when(z == 0)
    def _():
        for array in (KEY, VALUE):
            pass_on(array)
        for array in (QUERY, GRAD):
            pass_on(array)
        own_arrives()
        limit = limits(0, 0)
        score(0, 0, 0, 0, limit)
        value = pair_stat(0, 0)
        if key_back:
            key_arrives(1)
            score(1, 0, 1, 0, limit)
            value = merge(value, pair_stat(1, 0))
        finish(0, value)
        probs, score_grad = weights(0, 0, 0)
        acc_o[...] = dot(probs, buf[VALUE, 0], 0, 0)
        acc_q[...] = dot(score_grad, buf[KEY, 0], 0, 0)
        acc_v[...] = dot(probs, buf[GRAD, 0], 1, 0)
        acc_k[...] = dot(score_grad, buf[QUERY, 0], 1, 0)
        if key_back:
            probs, score_grad = weights(1, 0, 0)
            send_back(SIDE, DV, 0, 1, dot(probs, buf[GRAD, 0], 1, 0))
            send_back(SIDE, DK, 1, 1, dot(score_grad, buf[QUERY, 0], 1, 0))
            acc_o[...] += dot(probs, buf[VALUE, 1], 0, 0)
            acc_q[...] += dot(score_grad, buf[KEY, 1], 0, 0)
        send_result(DV, acc_v)
        send_result(DK, acc_k)
        send_result(OUT, acc_o)
        send_result(DQ, acc_q)
        emit(OUT)
        emit(DQ)

    @pl.when(z == 1)
    def _():
        for array in (QUERY, GRAD, KEY, VALUE):
            pass_on(array)
        own_arrives()
        score(0, 1, 1, 1, limits(1, 0))
        key_arrives(0)
        score(1, 1, 0, 1)
        send_stat(1, merge(pair_stat(0, 1), pair_stat(1, 1)))
        all_ready()

        def scores_of(block):
            query_arrives(block)
            score(1, block, 0, block)
            score(0, block, 1, block)
            send_stat(block, merge(pair_stat(0, block), pair_stat(1, block)))

        def query_side(far, far_grad, near, near_grad):
            return (
                dot(far, buf[VALUE, 0], 0, 0) + dot(near, buf[VALUE, 1], 0, 0),
                dot(far_grad, buf[KEY, 0], 0, 0) + dot(near_grad, buf[KEY, 1], 0, 0))

        alt[...] = jnp.zeros_like(alt)

        alt[...] = jnp.zeros_like(alt)

        def finish_block(block):
            settle(block)
            far, far_grad = weights(1, block, block)
            alt[0] += dot(far, buf[GRAD, block], 1, 0)
            alt[1] += dot(far_grad, buf[QUERY, block], 1, 0)
            near, near_grad = weights(0, block, block)
            output, query_grad = query_side(far, far_grad, near, near_grad)
            hold_back(OUT, 2 * block, output)
            hold_back(DQ, 2 * block + 1, query_grad)

        pl.loop(2, last)(scores_of)
        pl.loop(2, last)(finish_block)
        scores_of(last)
        @pl.loop(2, last)
        def _(block):
            for part, slot in enumerate((OUT, DQ)):
                for portion in range(HEADS):
                    ret_copy(HUB, slot, 2 * block + part, block, portion).start()
        settle(1)
        key_side(1, 1, 1, alt.at[0], alt.at[1])
        settle(last)
        far, far_grad = weights(1, last, last)
        for portion in range(HEADS):
            part = slice(portion * rows, (portion + 1) * rows)
            ret_out[0, part] = (alt[0, part] + dot(far[part], buf[GRAD, last], 1, 0)).astype(jnp.bfloat16)
            ret_copy(HUB, DV, 0, 0, portion).start()
            ret_out[1, part] = (
                (alt[1, part] + dot(far_grad[part], buf[QUERY, last], 1, 0)) * scaling).astype(jnp.bfloat16)
            ret_copy(HUB, DK, 1, 0, portion).start()
        near, near_grad = weights(0, last, last)
        output, query_grad = query_side(far, far_grad, near, near_grad)
        send_back(HUB, OUT, 2 * last, last, output)
        send_back(HUB, DQ, 2 * last + 1, last, query_grad)
        acc_v[...] = dot(near, buf[GRAD, last], 1, 0)
        acc_k[...] = dot(near_grad, buf[QUERY, last], 1, 0)

        far, far_grad = weights(1, 1, 1)
        near, near_grad = weights(0, 1, 1)
        acc_o[...], acc_q[...] = query_side(far, far_grad, near, near_grad)
        send_result(OUT, acc_o)
        send_result(DQ, acc_q)
        acc_v[...] += dot(near, buf[GRAD, 1], 1, 0)
        acc_k[...] += dot(near_grad, buf[QUERY, 1], 1, 0)

        @pl.loop(2, last)
        def _(block):
            key_side(0, block, block, acc_v, acc_k)
        send_result(DV, acc_v)
        send_result(DK, acc_k)

    @pl.when(z >= 2)
    def _():
        for array in (QUERY, GRAD, KEY, VALUE):
            pass_on(array)
        own_arrives()
        score(0, z, z, z, limits(z, 0))
        send_stat(z, pair_stat(0, z))

        @pl.when(ahead(z - 1))
        def _():
            query_arrives(z - 1)
            landed(ends.at[HEADS:2 * HEADS], end_recv)
            score(0, z - 1, z, z - 1, limits(z - 1, HEADS))
            send_stat(z - 1, pair_stat(0, z - 1))

        @pl.loop(z + 1, blocks)
        def _(block):
            query_arrives(block)
            score(0, block, z, block)
            send_stat(block, pair_stat(0, block))

        all_ready()
        acc_k[...] = jnp.zeros_like(acc_k)
        acc_v[...] = jnp.zeros_like(acc_v)
        @pl.when(ahead(z - 1))
        def _():
            settle(z - 1)
            probs, score_grad = weights(0, z - 1, z - 1)
            send_back(SIDE, OUT, 0, z - 1, dot(probs, buf[VALUE, z], 0, 0))
            send_back(SIDE, DQ, 1, z - 1, dot(score_grad, buf[KEY, z], 0, 0))
            acc_v[...] += dot(probs, buf[GRAD, z - 1], 1, 0)
            acc_k[...] += dot(score_grad, buf[QUERY, z - 1], 1, 0)

        @pl.loop(1, z - 1)
        def _(back):
            key_arrives(z - back)
            score(1, z - back, z - back, z)

        settle(z)
        probs, score_grad = weights(0, z, z)
        acc_v[...] += dot(probs, buf[GRAD, z], 1, 0)
        acc_k[...] += dot(score_grad, buf[QUERY, z], 1, 0)
        @pl.when(z == last)
        def _():
            send_result(DV, acc_v)
            send_result(DK, acc_k)
        acc_o[...] = dot(probs, buf[VALUE, z], 0, 0)
        acc_q[...] = dot(score_grad, buf[KEY, z], 0, 0)

        @pl.loop(1, z - 1)
        def _(back):
            block = z - back
            probs, score_grad = weights(1, block, z)
            acc_o[...] += dot(probs, buf[VALUE, block], 0, 0)
            acc_q[...] += dot(score_grad, buf[KEY, block], 0, 0)
        send_result(OUT, acc_o)
        send_result(DQ, acc_q)

        @pl.when(z < last)
        def _():
            @pl.loop(z + 1, blocks)
            def _(block):
                settle(block)
                key_side(0, block, block, acc_v, acc_k)
            send_result(DV, acc_v)
            send_result(DK, acc_k)

    @pl.when(z == 0)
    def _():
        all_ready()
    for _ in range(4):
        res_copy(0).wait_send()
        x_copy(0).wait_send()
    x_ends().wait_send()
    @pl.when(up_query)
    def _():
        for column in range(HEADS):
            up_ends(column).wait_send()
            for array in (QUERY, GRAD):
                query_copy(array, z + 1, column).wait_send()
    @pl.loop(1, z)
    def _(target):
        for _ in range(4):
            query_copy(QUERY, target, x).wait_send()
    @pl.when(down_key)
    def _():
        for _ in range(4):
            query_copy(KEY, 0, x).wait_send()
    @pl.loop(0, z + 1)
    def _(block):
        @pl.when(up_key(block))
        def _():
            for _ in range(4):
                array_copy(KEY, block, 0, z + 1).wait_send()
    @pl.when(z >= 1)
    def _():
        @pl.loop(jnp.maximum(z - 1, 1), blocks)
        def _(block):
            @pl.when((block >= z) | ahead(z - 1))
            def _():
                for target in range(1, blocks):
                    @pl.when(takes_part(block, target) & (target != z))
                    def _():
                        stat_copy(block, target).wait_send()
    @pl.when(((z == 0) & ahead(0)) | (z == 1) | ((z >= 2) & ahead(z - 1)))
    def _():
        for _ in range(4):
            ret_copy(HUB, OUT, 0, 0, 0).wait_send()
    @pl.when(z == 1)
    def _():
        @pl.loop(2, blocks)
        def _(block):
            for _ in range(4):
                ret_copy(HUB, OUT, 0, 0, 0).wait_send()

    @pl.when(z == 0)
    def _():
        emit(DV, HUB)
        emit(DK, HUB)
    @pl.when(z == 1)
    def _():
        for slot in (OUT, DQ):
            emit(slot, *((SIDE,) if query_back else ()))
        for slot in (DV, DK):
            emit(slot, *((SIDE,) if key_back else ()))
    @pl.when(z >= 2)
    def _():
        @pl.when(ahead(z))
        def _():
            emit(OUT, HUB, SIDE)
            emit(DQ, HUB, SIDE)
        @pl.when(jnp.logical_not(ahead(z)))
        def _():
            emit(OUT, HUB)
            emit(DQ, HUB)
        emit(DV)
        emit(DK)


def flush(*refs):
    sem = refs[-1]
    copies = [pltpu.make_async_copy(refs[i], refs[i + 4], sem) for i in range(4)]
    for copy in copies:
        copy.start()
    for copy in copies:
        copy.wait()


def solution(mesh):
    n = mesh.shape["ctx"]

    def local(queries, keys, values, out_grad, span_end):
        rows = queries.shape[0]
        blocks, span = n // HEADS, HEADS * rows
        f32, bf16 = jnp.float32, jnp.bfloat16
        anywhere = pl.BlockSpec(memory_space=pl.ANY)
        vmem = pl.BlockSpec(memory_space=pltpu.VMEM)
        dma = pltpu.SemaphoreType.DMA
        results = pl.pallas_call(
            functools.partial(kernel, n, rows),
            out_shape=tuple(
                pltpu.VMEM(queries.shape, kind) for kind in (bf16, f32, f32, f32)),
            in_specs=[anywhere] * 5,
            out_specs=(vmem,) * 4,
            scratch_shapes=[
                pltpu.VMEM((4, blocks, span, HEAD_DIM), bf16),
                pltpu.VMEM((2 * HEADS, 1, rows), jnp.int32),
                pltpu.VMEM((2, blocks, span, span), f32),
                pltpu.VMEM((2, blocks, span, span), f32),
                pltpu.VMEM((2, blocks, 3, span), f32),
                pltpu.VMEM((blocks, blocks, 3, span), f32),
                pltpu.VMEM((blocks, 3, span), f32),
                pltpu.VMEM((3, span), f32),
                pltpu.VMEM((blocks, 2, span), f32),
                pltpu.VMEM((span, HEAD_DIM), f32),
                pltpu.VMEM((span, HEAD_DIM), f32),
                pltpu.VMEM((span, HEAD_DIM), f32),
                pltpu.VMEM((span, HEAD_DIM), f32),
                pltpu.VMEM((2, span, HEAD_DIM), f32),
                pltpu.VMEM((2 * blocks, span, HEAD_DIM), bf16),
                pltpu.VMEM((2, 4, HEADS, rows, HEAD_DIM), bf16),
                pltpu.VMEM((4, rows, HEAD_DIM), bf16),
                pltpu.VMEM((4, rows, HEAD_DIM), bf16),
                dma((2,)),
                dma((5,)),
                dma((2, blocks)),
                dma,
                dma((blocks - 1, blocks - 1)),
                dma((2, 4)),
                dma((4,)),
                dma,
                pltpu.SemaphoreType.REGULAR((blocks - 1,)),
            ],
            compiler_params=pltpu.CompilerParams(collective_id=0, has_side_effects=True),
        )(queries, keys, values, out_grad, span_end[None])
        return pl.pallas_call(
            flush,
            out_shape=tuple(
                jax.ShapeDtypeStruct(queries.shape, kind) for kind in (bf16, f32, f32, f32)),
            in_specs=[vmem] * 4,
            out_specs=(anywhere,) * 4,
            scratch_shapes=[dma],
        )(*(pltpu.with_memory_space_constraint(result, pltpu.VMEM) for result in results))

    spec = P(("dp", "ctx"), None)
    return jax.shard_map(
        local, mesh=mesh, in_specs=(spec,) * 4 + (P(("dp", "ctx")),),
        out_specs=(spec,) * 4, check_vma=False)
```
